256 devices in a mesh: gx: 4 (over y), gy: 8 (over x, core), gz: 8 (over z).
Axes of the slice: x: 4, y: 4, z: 8, core: 2. Of those that a mesh axis runs over, the one named last changes fastest.
Arguments:
- basis: bfloat16 [8, 3, 64, 1024, 128], P('gx', None, 'gy', 'gz'), may hold values from -4.8 to 4.8
- modal_now: bfloat16 [128, 8], replicated, may hold values from -0.5 to 0.5
- modal_prev: bfloat16 [128, 8], replicated, may hold values from -0.5 to 0.5
- material_ids: int32 [8, 64, 1024], P('gx', 'gy', 'gz'), may hold values from 0 to 3
- moduli: float32 [3, 4], replicated, may hold values from 0.4 to 1.6
- drive_mask: int32 [8, 8, 64, 1024], P(None, 'gx', 'gy', 'gz'), may hold values 0 or 1
- drive: float32 [3, 8], replicated, may hold values from -8 to 8
Outputs:
- displacement: float32 [3, 8, 8, 64, 1024], P(None, None, 'gx', 'gy', 'gz')
- modes: float32 [3, 8, 8, 64, 1024], P(None, None, 'gx', 'gy', 'gz')
- coefficients: float32 [4, 2, 128, 8], replicated
- rfactor: float32 [4, 8, 8], replicated
The draws below stay inside these ranges and needn't reach their ends.
All inputs are finite; a program needn't handle non-finite values. No bound on the sum of `drive_mask` on one device may be relied on, other than what follows from the above.
Results may differ from the reference program's by a relative error of at most 0.0008.
The reference program's roundings to bfloat16 on the way (of `snapshot`) count: a program that leaves them out, or rounds other values in their place, can miss the bound.
Values sent between devices are 32-bit elements; how exact they have to be, the bound alone decides.
No kernel may reach another device: no remote copies, remote signals or barrier semaphores. Data moves between devices by JAX's collectives and lax.ppermute only.
A program may use at most 128 MiB of HBM per device.

```python
import math
import jax
import jax.numpy as jnp
from jax import lax

MODES = 128
CASES = 8
NMAT = 4
STEPS = 4
NX = 8
NY = 64
NZ = 1024


def draw_basis(key, part):
    first_key, second_key = jax.random.split(jax.random.fold_in(key, 11))
    shape = (NX, 3, NY, NZ, MODES)
    scales = 0.8 + 0.4 * jax.random.uniform(second_key, (MODES,), jnp.float32)
    values = jax.random.truncated_normal(first_key, -4.0, 4.0, shape, jnp.float32)
    return (values * scales).astype(jnp.bfloat16)


def place_ends(values, stream_key, least, high):
    spot = [jax.random.randint(jax.random.fold_in(stream_key, axis), (), 0, length) for axis, length in enumerate(values.shape)]
    longest = values.shape.index(max(values.shape))
    next_to = spot[:longest] + [(spot[longest] + 1) % values.shape[longest]] + spot[longest + 1:]
    return values.at[tuple(spot)].set(least).at[tuple(next_to)].set(high)


def bell_draw(rng, dims, spread, limit, held_as=jnp.bfloat16):
    values = jax.random.normal(rng, dims, jnp.float32) * spread
    return jnp.minimum(jnp.maximum(values, -limit), limit).astype(held_as)


def setup_inputs(seed: int = 0) -> dict:
    key_of = jax.random.split(jax.random.key(seed), 8)
    return {
        "basis": draw_basis(jax.random.fold_in(key_of[7], 71), 0),
        "modal_now": bell_draw(key_of[1], (MODES, CASES), MODES ** -0.5, 0.5),
        "modal_prev": bell_draw(key_of[2], (MODES, CASES), MODES ** -0.5, 0.5),
        "material_ids": place_ends(jax.random.randint(key_of[3], (NX, NY, NZ), 0, NMAT), jax.random.fold_in(key_of[3], 1), 0, NMAT - 1).astype(jnp.int32),
        "moduli": jnp.clip(jnp.exp(jax.random.uniform(key_of[4], (3, NMAT), jnp.float32, math.log(0.4), math.log(1.6))), 0.4, 1.6),
        "drive_mask": place_ends((jax.random.randint(key_of[5], (CASES, NX, NY, NZ), 0, 8) < 1).astype(jnp.int32), jax.random.fold_in(key_of[5], 1), 0, 1),
        "drive": bell_draw(key_of[6], (3, CASES), 2.0, 8.0, jnp.float32),
    }


step_squared = 0.1
ramp_steps = 4.0

def interior(array, direction_axis, offset):
    base_axis = array.ndim - 3
    result = array
    for axis_index in range(3):
        extent = array.shape[base_axis + axis_index]
        begin = offset if axis_index == direction_axis else 1
        result = lax.slice_in_dim(result, begin, extent - 2 + begin, axis=base_axis + axis_index)
    return result

def stiffness(field, material_props):
    component_rows = []
    for component in range(3):
        center = interior(field[component], 0, 1)
        accumulated = jnp.zeros_like(center)
        for direction_axis in range(3):
            modulus = material_props[0] if component == direction_axis else material_props[1]
            center_modulus = interior(modulus, 0, 1)
            for offset in (0, 2):
                coupling = 0.5 * (center_modulus + interior(modulus, direction_axis, offset))
                accumulated = accumulated + coupling * (center - interior(field[component], direction_axis, offset))
        component_rows.append(accumulated)
    return jnp.stack(component_rows)

def lookup(material_ids, moduli):
    levels = jnp.arange(moduli.shape[1], dtype=jnp.int32)
    onehot = (material_ids[None] == levels[:, None, None, None]).astype(moduli.dtype)
    return jnp.einsum('mxyz,pm->pxyz', onehot, moduli, precision=lax.Precision.HIGHEST)

def expand(basis, coefficient):
    weights = coefficient.astype(jnp.float32)

    def per_slab(basis_slab):
        return jnp.einsum('cyzk,kj->cjyz', basis_slab.astype(jnp.float32), weights, precision=lax.Precision.HIGHEST)
    slabs = lax.map(per_slab, basis)
    return jnp.moveaxis(slabs, 0, 2)

def project(basis, field):
    moved = jnp.moveaxis(field, 2, 0)

    def per_slab(running, pair_slabs):
        basis_slab, field_slab = pair_slabs
        return (running + jnp.einsum('cyzk,cjyz->kj', basis_slab.astype(jnp.float32), field_slab.astype(jnp.float32), precision=lax.Precision.HIGHEST), None)
    start = jnp.zeros((basis.shape[4], field.shape[1]), jnp.float32)
    running, unused = lax.scan(per_slab, start, (basis, moved))
    return running

def gram_of(block, dof_weight):
    return jnp.einsum('cixyz,cjxyz->ij', block, block, precision=lax.Precision.HIGHEST) * dof_weight

def apply_inverse(block, lower_factor):
    identity_block = jnp.eye(lower_factor.shape[0], dtype=lower_factor.dtype)
    lower_inverse = jax.scipy.linalg.solve_triangular(lower_factor, identity_block, lower=True)
    return jnp.einsum('cixyz,ji->cjxyz', block, lower_inverse, precision=lax.Precision.HIGHEST)

def reference(basis, modal_now, modal_prev, material_ids, moduli, drive_mask, drive):
    dof_weight = 1.0 / (3.0 * NX * NY * NZ)
    current = expand(basis, modal_now)
    earlier = expand(basis, modal_prev)
    material_props = lookup(material_ids, moduli)
    props_padded = jnp.pad(material_props, ((0, 0), (1, 1), (1, 1), (1, 1)))
    port_mask = drive_mask.astype(jnp.float32)
    coefficient_list = []
    factor_list = []
    modes = current
    for step in range(STEPS):
        ramp_level = min(1.0, (step + 1) / ramp_steps)
        padded = jnp.pad(current, ((0, 0), (0, 0), (1, 1), (1, 1), (1, 1)))
        load_field = drive[:, :, None, None, None] * port_mask[None] * ramp_level
        following = 2.0 * current - earlier + step_squared * material_props[2] * (load_field - stiffness(padded, props_padded))
        earlier = current
        current = following
        snapshot = following.astype(jnp.bfloat16)
        first_coef = project(basis, snapshot) * dof_weight
        first_resid = snapshot.astype(jnp.float32) - expand(basis, first_coef.astype(jnp.bfloat16))
        first_lower = jnp.linalg.cholesky(gram_of(first_resid, dof_weight))
        first_q = apply_inverse(first_resid, first_lower)
        second_coef = project(basis, first_q.astype(jnp.bfloat16)) * dof_weight
        second_resid = first_q - expand(basis, second_coef.astype(jnp.bfloat16))
        second_lower = jnp.linalg.cholesky(gram_of(second_resid, dof_weight))
        modes = apply_inverse(second_resid, second_lower)
        coefficient_list.append(jnp.stack([first_coef, second_coef]))
        factor_list.append(jnp.dot(first_lower, second_lower, precision=lax.Precision.HIGHEST).T)
    return (current, modes, jnp.stack(coefficient_list), jnp.stack(factor_list))
```

```python
import jax
import jax.numpy as jnp
from jax import lax
from jax.sharding import PartitionSpec as P

STEPS = 4
CASES = 8


step_squared = 0.1
ramp_steps = 4.0


def padded_2(block, sides, width):
    for axis, dim in sides:
        count = lax.axis_size(axis)
        forward = [(i, i + 1) for i in range(count - 1)]
        backward = [(target, source) for source, target in forward]
        low = lax.ppermute(
            lax.slice_in_dim(block, block.shape[dim] - width, None, axis=dim), axis, forward
        )
        high = lax.ppermute(lax.slice_in_dim(block, 0, width, axis=dim), axis, backward)
        block = jnp.concatenate([low, block, high], axis=dim)
    return block


def interior(array, direction_axis, offset):
    base_axis = array.ndim - 3
    result = array
    for axis_index in range(3):
        extent = array.shape[base_axis + axis_index]
        begin = offset if axis_index == direction_axis else 1
        result = lax.slice_in_dim(result, begin, extent - 2 + begin, axis=base_axis + axis_index)
    return result


def stiffness(field, material_props):
    component_rows = []
    for component in range(3):
        center = interior(field[component], 0, 1)
        accumulated = jnp.zeros_like(center)
        for direction_axis in range(3):
            modulus = material_props[0] if component == direction_axis else material_props[1]
            center_modulus = interior(modulus, 0, 1)
            for offset in (0, 2):
                coupling = 0.5 * (center_modulus + interior(modulus, direction_axis, offset))
                accumulated = accumulated + coupling * (
                    center - interior(field[component], direction_axis, offset)
                )
        component_rows.append(accumulated)
    return jnp.stack(component_rows)


def lookup(material_ids, moduli):
    levels = jnp.arange(moduli.shape[1], dtype=jnp.int32)
    onehot = (material_ids[None] == levels[:, None, None, None]).astype(jnp.float32)
    return jnp.einsum("mxyz,pm->pxyz", onehot, moduli, precision=lax.Precision.HIGHEST)


def expand(basis, coefficient):
    return jnp.einsum("xcyzk,kj->cjxyz", basis, coefficient, preferred_element_type=jnp.float32)


def dot_f32(a, b, contract):
    return lax.dot_general(
        a, b, ((contract[:1], contract[1:]), ((), ())),
        precision=lax.Precision.HIGHEST, preferred_element_type=jnp.float32,
    )


def factor(gram):
    rows = lax.broadcasted_iota(jnp.int32, (CASES, 2 * CASES), 0)
    cols = lax.broadcasted_iota(jnp.int32, (CASES, 2 * CASES), 1)
    work = jnp.concatenate(
        [gram, (rows[:, :CASES] == cols[:, :CASES]).astype(jnp.float32)], axis=1
    )
    for p in range(CASES):
        scale = 1.0 / jnp.sqrt(work[p : p + 1, p : p + 1])
        row = work[p : p + 1] * scale
        below = jnp.where(rows[:, :1] > p, work[:, p : p + 1] * scale, 0.0)
        work = jnp.where(rows == p, row, work - below * row)
    upper = jnp.where(rows[:, :CASES] <= cols[:, :CASES], work[:, :CASES], 0.0)
    return upper, work[:, CASES:]


def gather_sum(part, axis):
    count = lax.axis_size(axis)
    spread = jnp.broadcast_to(part[None], (count,) + part.shape)
    return lax.all_to_all(spread, axis, 0, 0, tiled=True)


def reduced(coefs, squares, gram, weight):
    modes = gram.shape[0]
    slabs = lax.axis_size("gx")
    quarter = lax.all_to_all(gram.reshape(slabs, modes // slabs, modes), "gx", 0, 0, tiled=True)
    part = jnp.concatenate([coefs, jnp.pad(squares, ((0, 0), (0, modes - squares.shape[1]))), quarter.sum(0)])
    part = gather_sum(part, "gy").sum(0)
    part = gather_sum(part, "gz").sum(0)
    parts = gather_sum(part, "gx")
    n = coefs.shape[0]
    own = parts[:, : 2 * n].sum(0) * weight
    gram = parts[:, 2 * n :].reshape(modes, modes) * weight
    return own[:n], own[n:, :n], gram


def small_math(coef, squares, gram):
    rounded = lax.reduce_precision(coef, 8, 7)
    left = coef - dot_f32(rounded, gram, (1, 0))
    first = squares - dot_f32(coef, rounded, (1, 1)) - dot_f32(rounded, left, (1, 1))
    upper_1, inverse_1, second_list = [], [], []
    for s in range(STEPS):
        at = slice(s * CASES, (s + 1) * CASES)
        upper, inverse = factor(first[at, at])
        upper_1.append(upper)
        inverse_1.append(inverse)
        second_list.append(dot_f32(inverse, left[at], (1, 0)))
    second = jnp.concatenate(second_list)
    rounded_2 = lax.reduce_precision(second, 8, 7)
    left_2 = second - dot_f32(rounded_2, gram, (1, 0))
    change = dot_f32(second, rounded_2, (1, 1)) + dot_f32(rounded_2, left_2, (1, 1))
    factors = []
    for s in range(STEPS):
        at = slice(s * CASES, (s + 1) * CASES)
        whole = dot_f32(dot_f32(inverse_1[s], first[at, at], (1, 0)), inverse_1[s], (1, 1))
        upper, inverse = factor(whole - change[at, at])
        factors.append(dot_f32(upper, upper_1[s], (1, 0)))
    mix = dot_f32(inverse, inverse_1[-1], (1, 0))
    shift = dot_f32(mix, rounded[at], (1, 0)) + dot_f32(inverse, rounded_2[at], (1, 0))
    coefficients = jnp.stack([coef, second]).reshape(2, STEPS, CASES, -1).transpose(1, 0, 3, 2)
    return coefficients, jnp.stack(factors), mix, shift


def shards(basis, modal_now, modal_prev, material_ids, moduli, drive_mask, drive):
    devices_total = lax.axis_size("gx") * lax.axis_size("gy") * lax.axis_size("gz")
    dof_weight = 1.0 / (3.0 * basis.shape[0] * basis.shape[2] * basis.shape[3] * devices_total)
    current = expand(basis, modal_now)
    earlier = expand(basis, modal_prev)
    material_props = lookup(material_ids, moduli)
    port_mask = drive_mask.astype(jnp.float32)
    static = jnp.concatenate([material_props, port_mask], axis=0)
    wide_static = padded_2(static, (("gx", 1), ("gy", 2), ("gz", 3)), 2)
    props_wide = wide_static[:3]
    props_near = props_wide[:, 1:-1, 1:-1, 1:-1]
    inverse_mass = material_props[2]
    drive_field = drive[:, :, None, None, None]
    snapshots = []
    for step in range(STEPS):
        padded = padded_2(current, (("gx", 2), ("gy", 3), ("gz", 4)), 1)
        ramp_level = min(1.0, (step + 1) / ramp_steps)
        load_field = drive_field * port_mask[None] * ramp_level
        following = (
            2.0 * current
            - earlier
            + step_squared * inverse_mass * (load_field - stiffness(padded, props_near))
        )
        earlier = current
        current = following
        snapshots.append(following.astype(jnp.bfloat16))
    fields = jnp.concatenate(snapshots, axis=1)
    coefs = jnp.einsum("xcyzk,cjxyz->jk", basis, fields, preferred_element_type=jnp.float32)
    squares = jnp.einsum("cixyz,cjxyz->ij", fields, fields, preferred_element_type=jnp.float32)
    rows = basis.reshape(-1, basis.shape[-1])
    gram = jnp.einsum("nk,nl->kl", rows, rows, preferred_element_type=jnp.float32)
    coefs, squares, gram = reduced(coefs, squares, gram, dof_weight)
    coefficients, factors, mix, shift = small_math(coefs, squares, gram)
    last = snapshots[-1].astype(jnp.float32)
    modes = jnp.einsum("cixyz,ji->cjxyz", last, mix, precision=lax.Precision.HIGHEST)
    for _ in range(3):
        part = lax.reduce_precision(shift, 8, 7)
        shift = shift - part
        modes = modes - expand(basis, part.astype(jnp.bfloat16).T)
    return (current, modes, coefficients, factors)


def solution(mesh):
    in_specs = (
        P("gx", None, "gy", "gz", None),
        P(),
        P(),
        P("gx", "gy", "gz"),
        P(),
        P(None, "gx", "gy", "gz"),
        P(),
    )
    out_specs = (P(None, None, "gx", "gy", "gz"), P(None, None, "gx", "gy", "gz"), P(), P())
    return jax.shard_map(shards, mesh=mesh, in_specs=in_specs, out_specs=out_specs, check_vma=False)
```

```python
import jax
import jax.numpy as jnp
from jax import lax
from jax.experimental import pallas as pl
from jax.experimental.pallas import tpu as pltpu
from jax.sharding import PartitionSpec as P

STEPS = 4
CASES = 8
step_squared = 0.1
ramp_steps = 4.0

PAIR = 2
FIELDS = 3 * PAIR
MASKS = 2 * FIELDS
MATERIAL = MASKS + PAIR
COUNT = MATERIAL + 1
EDGE = 2 * COUNT
GRAM = EDGE + 2
REACH = 4
f32 = jnp.float32
bf16 = jnp.bfloat16


def dot(a, b, contract, precision=None):
    return lax.dot_general(
        a, b, ((contract[:1], contract[1:]), ((), ())),
        precision=precision, preferred_element_type=f32,
    )


def lanes_of(shape):
    return lax.broadcasted_iota(jnp.int32, shape, len(shape) - 1)


def rows_of(shape):
    return lax.broadcasted_iota(jnp.int32, shape, len(shape) - 2)


def start_kernel(now, prev, basis, ids, mask, out, down, up, stage):
    modal = jnp.concatenate([now[...].astype(f32), prev[...].astype(f32)], axis=1).T.astype(bf16)
    layers, comps, ny, nz, modes = basis.shape
    slabs = out.shape[0]
    gram = jnp.zeros((modes, modes), f32)
    for x in range(layers):
        for c in range(comps):
            rows = basis[x, c].reshape(ny * nz, modes)
            both = dot(modal, rows, (1, 1))
            at = x * comps + c
            for y in range(ny):
                stage[at, pl.ds(y, 2 * CASES, stride=ny), :] = both[:, y * nz : (y + 1) * nz]
            for r in range(2 * CASES):
                j = r % CASES
                field = (r // CASES) * FIELDS + (j % PAIR) * comps + c
                out[j // PAIR, 2 * field + x] = stage[at, r * ny : (r + 1) * ny, :]
            gram = gram + dot(rows, rows, (0, 0))
    share = modes // slabs
    for p in range(slabs):
        for x in range(layers):
            for i in range(PAIR):
                out[p, 2 * (MASKS + i) + x] = mask[PAIR * p + i, x].astype(f32)
            out[p, 2 * MATERIAL + x] = (ids[x] + 1).astype(f32)
        for t in range(share // 8):
            out[p, GRAM + t] = gram[share * p + 8 * t : share * p + 8 * t + 8]
        quarter = lanes_of((ny, nz)) // REACH
        for t in range(2):
            low = jnp.zeros((ny, nz), f32)
            high = jnp.zeros((ny, nz), f32)
            for g in range(16):
                tile = 16 * t + g
                if tile < 2 * COUNT:
                    v = out[p, tile]
                    low = jnp.where(quarter == 2 * g, pltpu.roll(v, 8 * g, 1) if g else v, low)
                    turn = (8 * g + 8) % nz
                    high = jnp.where(quarter == 2 * g + 1, pltpu.roll(v, turn, 1) if turn else v, high)
            down[p, t] = low
            up[p, t] = high
            out[p, EDGE + t] = jnp.zeros((ny, nz), f32)


def faces_kernel(block, down, up):
    slabs = block.shape[0]
    first = rows_of(block.shape[2:]) < REACH
    for g in range(slabs):
        for q in range(COUNT + 1):
            a = block[g, 2 * q]
            b = pltpu.roll(block[g, 2 * q + 1], REACH, 0)
            down[g, q] = jnp.where(first, a, b)
            up[g, q] = jnp.where(first, b, a)


def steps_kernel(place, drive, moduli, block, above, below, out, share, fields, masks, stiff, weight, couple, diagonal):
    slabs, _, ny, nz = block.shape
    nx = 2 * slabs
    first = rows_of((ny, nz)) < REACH
    lane = lanes_of((ny, nz))
    zero = jnp.zeros((ny, nz), f32)
    wide_zero = jnp.zeros((2 * ny, 2 * nz), f32)
    for g in range(slabs):
        edges = [
            (block[g, EDGE], jnp.where(first, above[g, COUNT], below[g, COUNT])),
            (block[g, EDGE + 1], pltpu.roll(jnp.where(first, below[g, COUNT], above[g, COUNT]), REACH, 0)),
        ]
        for q in range(COUNT):
            beside = (
                jnp.where(first, above[g, q], below[g, q]),
                pltpu.roll(jnp.where(first, below[g, q], above[g, q]), REACH, 0),
            )
            for i in range(2):
                x = 2 * g + i
                spot = 2 * q + i
                ends = []
                for edge in edges[spot // 16]:
                    turn = 8 * (spot % 16)
                    right = pltpu.roll(edge, (nz - turn) % nz, 1) if turn else edge
                    left = pltpu.roll(edge, (2 * nz - 8 - turn) % nz, 1) if (nz - 8 - turn) % nz else edge
                    ends.append(jnp.where(lane < REACH, right, jnp.where(lane >= nz - REACH, left, zero)))
                parts = ((block[g, spot], ends[0]), (beside[i], ends[1]))
                for k in range(2):
                    for h in range(2):
                        here = (slice(k * ny, (k + 1) * ny), slice(h * nz, (h + 1) * nz))
                        value = parts[k][h]
                        if q < FIELDS:
                            fields[0, q, 1 + x, here[0], here[1]] = value
                        elif q < MASKS:
                            fields[1, q - FIELDS, 1 + x, here[0], here[1]] = value
                        elif q < MATERIAL:
                            masks[q - MASKS, x, here[0], here[1]] = value
                        else:
                            for prop in range(3):
                                level = zero
                                for m in range(moduli.shape[1]):
                                    level = jnp.where(value == m + 1.0, moduli[prop, m], level)
                                if prop < 2:
                                    stiff[prop, 1 + x, here[0], here[1]] = level
                                else:
                                    weight[x, here[0], here[1]] = step_squared * level
    for x in (0, nx + 1):
        for f in range(FIELDS):
            fields[0, f, x] = wide_zero
            fields[1, f, x] = wide_zero
        stiff[0, x] = wide_zero
        stiff[1, x] = wide_zero
    for t in range(share.shape[0]):
        total = block[0, GRAM + t]
        for g in range(1, slabs):
            total = total + block[g, GRAM + t]
        share[t] = total

    def beside_of(ref, lead, x):
        v = ref[lead + (x + 1,)]
        return v, (
            ref[lead + (x,)], ref[lead + (x + 2,)],
            pltpu.roll(v, 1, 0), pltpu.roll(v, 2 * ny - 1, 0),
            pltpu.roll(v, 1, 1), pltpu.roll(v, 2 * nz - 1, 1),
        )

    def prepare(x, carry):
        half = 0.5 * weight[x]
        sums = []
        for kind in range(2):
            v, near = beside_of(stiff, (kind,), x)
            pairs = []
            for d in range(6):
                value = half * (v + near[d])
                couple[kind, d, x] = value
                pairs.append(value)
            sums.append([pairs[2 * a] + pairs[2 * a + 1] for a in range(3)])
        for c in range(3):
            total = sums[0][c] + sums[1][(c + 1) % 3] + sums[1][(c + 2) % 3]
            diagonal[c, x] = 2.0 - total
        for i in range(PAIR):
            masks[i, x] = masks[i, x] * weight[x]
        return carry

    lax.fori_loop(0, nx, prepare, 0)
    slab = place[0]
    for s in range(STEPS):
        ramp = min(1.0, (s + 1) / ramp_steps)

        def step(x, carry):
            for i in range(PAIR):
                for c in range(3):
                    f = 3 * i + c
                    v, near = beside_of(fields, (s % 2, f), x)
                    value = diagonal[c, x] * v - fields[1 - s % 2, f, x + 1]
                    value = value + masks[i, x] * (drive[c, PAIR * slab + i] * ramp)
                    for d in range(6):
                        kind = 0 if d // 2 == c else 1
                        value = value + couple[kind, d, x] * near[d]
                    fields[1 - s % 2, f, x + 1] = value
                    out[x // 2, s, f, x % 2] = value[:ny, :nz]
            return carry

        lax.fori_loop(0, nx, step, 0)


def project_kernel(basis, states, share, out, stage):
    layers, comps, ny, nz, modes = basis.shape
    count = STEPS * CASES
    coef = jnp.zeros((count, modes), f32)
    square = jnp.zeros((count, count), f32)
    for x in range(layers):
        for c in range(comps):
            at = x * comps + c
            for s in range(STEPS):
                for j in range(CASES):
                    r = s * CASES + j
                    stage[at, r * ny : (r + 1) * ny, :] = states[j // PAIR, s, (j % PAIR) * comps + c, x]
            block = jnp.concatenate(
                [stage[at, pl.ds(y, count, stride=ny), :].astype(bf16) for y in range(ny)], axis=1
            )
            coef = coef + dot(block, basis[x, c].reshape(ny * nz, modes), (1, 0))
            square = square + dot(block, block, (1, 1))
    lane = lanes_of((CASES, count))
    tile = jnp.zeros((CASES, count), f32)
    for s in range(STEPS):
        tile = jnp.where(lane // CASES == s, square[s * CASES : (s + 1) * CASES], tile)
    tile = jnp.concatenate([tile, jnp.zeros((CASES, modes - count), f32)], axis=1)
    for g in range(out.shape[0]):
        out[g, :count] = coef
        out[g, count : count + CASES] = tile
        for t in range(share.shape[0]):
            out[g, count + CASES + 8 * t : count + CASES + 8 * t + 8] = share[t]


def sum_kernel(parts, out):
    total = parts[0]
    for g in range(1, parts.shape[0]):
        total = total + parts[g]
    for g in range(out.shape[0]):
        out[g] = total


def factor(gram):
    rows = rows_of(gram.shape)
    lane = lanes_of(gram.shape)
    work = jnp.where(lane < CASES, gram, jnp.where(lane == rows + CASES, 1.0, 0.0))
    for p in range(CASES):
        scale = 1.0 / jnp.sqrt(work[p : p + 1, p : p + 1])
        row = work[p : p + 1] * scale
        below = jnp.where(rows[:, :1] > p, work[:, p : p + 1] * scale, 0.0)
        work = jnp.where(rows == p, row, work - below * row)
    upper = jnp.where((rows <= lane) & (lane < CASES), work, 0.0)
    inverse = jnp.where(lane < CASES, pltpu.roll(work, gram.shape[1] - CASES, 1), 0.0)
    return upper, inverse


def mixed(small, rows):
    total = small[:, :1] * rows[:1]
    for i in range(1, CASES):
        total = total + small[:, i : i + 1] * rows[i : i + 1]
    return total


def padded(rows):
    return jnp.concatenate([rows, jnp.zeros((rows.shape[1] - rows.shape[0], rows.shape[1]), f32)])


def finish_kernel(weight, parts, basis, states, displacement, modes_out, coefficients, factors, stage):
    layers, comps, ny, nz, modes = basis.shape
    count = STEPS * CASES
    high = lax.Precision.HIGHEST
    own = parts[0, : count + CASES]
    for g in range(1, parts.shape[0]):
        own = own + parts[g, : count + CASES]
    own = own * weight
    gram = jnp.concatenate([parts[g, count + CASES :] for g in range(parts.shape[0])]) * weight
    coef, square = own[:count], own[count:]
    lane = lanes_of(square.shape)

    def block_of(rows, s):
        turn = (modes - s * CASES) % modes
        rows = pltpu.roll(rows, turn, 1) if turn else rows
        return jnp.where(lane < CASES, rows, 0.0)

    rounded = coef.astype(bf16).astype(f32)
    left = coef - dot(rounded, gram, (1, 0), high)
    change = dot(coef, padded(rounded), (1, 1), high) + dot(rounded, padded(left), (1, 1), high)
    first, second = [], []
    for s in range(STEPS):
        at = slice(s * CASES, (s + 1) * CASES)
        first.append(factor(block_of(square - change[at], s)))
        second.append(mixed(first[s][1], left[at]))
    second = jnp.concatenate(second)
    rounded_2 = second.astype(bf16).astype(f32)
    left_2 = second - dot(rounded_2, gram, (1, 0), high)
    change = dot(second, padded(rounded_2), (1, 1), high) + dot(rounded_2, padded(left_2), (1, 1), high)
    for s in range(STEPS):
        at = slice(s * CASES, (s + 1) * CASES)
        whole = dot(first[s][0], padded(first[s][1]), (1, 1), high)
        upper, inverse = factor(whole - block_of(change[at], s))
        factors[s] = mixed(upper, first[s][0])[:, :CASES]
        coefficients[s, 0] = coef[at].T
        coefficients[s, 1] = second[at].T
    mix = mixed(inverse, first[-1][1])
    shift = mixed(mix, rounded[at]) + mixed(inverse, rounded_2[at])
    pieces = []
    for _ in range(3):
        piece = shift.astype(bf16)
        pieces.append(piece.astype(f32))
        shift = shift - piece.astype(f32)
    pieces = jnp.concatenate(pieces).astype(bf16)
    scalars = [[mix[i : i + 1, j : j + 1] for j in range(CASES)] for i in range(CASES)]
    for x in range(layers):
        for c in range(comps):
            at = x * comps + c
            taken = dot(pieces, basis[x, c].reshape(ny * nz, modes), (1, 1))
            taken = taken[:CASES] + taken[CASES : 2 * CASES] + taken[2 * CASES :]
            for y in range(ny):
                stage[at, pl.ds(y, CASES, stride=ny), :] = taken[:, y * nz : (y + 1) * nz]
            final = [states[j // PAIR, STEPS - 1, (j % PAIR) * comps + c, x] for j in range(CASES)]
            snapshot = [v.astype(bf16).astype(f32) for v in final]
            for i in range(CASES):
                displacement[c, i, x] = final[i]
                total = scalars[i][0] * snapshot[0]
                for j in range(1, CASES):
                    total = total + scalars[i][j] * snapshot[j]
                modes_out[c, i, x] = total - stage[at, i * ny : (i + 1) * ny, :]


def call(kernel, outs, inputs, scratch=(), scalars=0):
    vmem = pl.BlockSpec(memory_space=pltpu.VMEM)
    smem = pl.BlockSpec(memory_space=pltpu.SMEM)
    return pl.pallas_call(
        kernel,
        out_shape=[jax.ShapeDtypeStruct(shape, f32) for shape in outs],
        in_specs=[smem] * scalars + [vmem] * (len(inputs) - scalars),
        out_specs=[vmem] * len(outs),
        scratch_shapes=[pltpu.VMEM(shape, f32) for shape in scratch],
        compiler_params=pltpu.CompilerParams(vmem_limit_bytes=40 << 20),
    )(*inputs)


def sent(block, axis, forward):
    count = lax.axis_size(axis)
    pairs = [(i, i + 1) for i in range(count - 1)]
    return lax.ppermute(block, axis, pairs if forward else [(b, a) for a, b in pairs])


def turned(parts, axis):
    return lax.all_to_all(parts, axis, 0, 0, tiled=True)


def shards(basis, modal_now, modal_prev, material_ids, moduli, drive_mask, drive):
    layers, comps, ny, nz, modes = basis.shape
    slabs, rows, depth = (lax.axis_size(a) for a in ("gx", "gy", "gz"))
    dof_weight = 1.0 / (3.0 * layers * ny * nz * slabs * rows * depth)
    tile = (ny, nz)
    share = modes // slabs // 8
    blocks = layers * comps
    block, down, up = call(
        start_kernel,
        [(slabs, GRAM + share) + tile, (slabs, 2) + tile, (slabs, 2) + tile],
        [modal_now, modal_prev, basis, material_ids, drive_mask],
        [(blocks, 2 * CASES * ny, nz)],
    )
    edge = sent(down, "gz", False) + sent(up, "gz", True)
    block = turned(lax.dynamic_update_slice(block, edge, (0, EDGE, 0, 0)), "gx")
    down, up = call(faces_kernel, [(slabs, COUNT + 1) + tile] * 2, [block])
    above, below = sent(down, "gy", False), sent(up, "gy", True)
    nx = layers * slabs
    wide = (2 * ny, 2 * nz)
    place = lax.axis_index("gx").astype(jnp.int32)[None]
    states, gram = call(
        steps_kernel,
        [(slabs, STEPS, FIELDS, layers) + tile, (share,) + tile],
        [place, drive, moduli, block, above, below],
        [
            (2, FIELDS, nx + 2) + wide, (PAIR, nx) + wide, (2, nx + 2) + wide, (nx,) + wide,
            (2, 6, nx) + wide, (3, nx) + wide,
        ],
        3,
    )
    states = turned(states, "gx")
    count = STEPS * CASES
    width = count + CASES + 8 * share
    parts, = call(
        project_kernel, [(rows, width, modes)], [basis, states, gram], [(blocks, count * ny, nz)]
    )
    parts, = call(sum_kernel, [(depth, width, modes)], [turned(parts, "gy")])
    parts, = call(sum_kernel, [(slabs, width, modes)], [turned(parts, "gz")])
    return call(
        lambda *refs: finish_kernel(dof_weight, *refs),
        [(comps, CASES, layers) + tile] * 2 + [(STEPS, 2, modes, CASES), (STEPS, CASES, CASES)],
        [turned(parts, "gx"), basis, states],
        [(blocks, CASES * ny, nz)],
    )


def solution(mesh):
    in_specs = (
        P("gx", None, "gy", "gz", None),
        P(),
        P(),
        P("gx", "gy", "gz"),
        P(),
        P(None, "gx", "gy", "gz"),
        P(),
    )
    out_specs = (P(None, None, "gx", "gy", "gz"), P(None, None, "gx", "gy", "gz"), P(), P())
    return jax.shard_map(
        lambda *args: tuple(shards(*args)), mesh=mesh, in_specs=in_specs, out_specs=out_specs, check_vma=False
    )
```

```python
import jax
import jax.numpy as jnp
from jax import lax
from jax.experimental import pallas as pl
from jax.experimental.pallas import tpu as pltpu
from jax.sharding import PartitionSpec as P

STEPS = 4
CASES = 8
step_squared = 0.1
ramp_steps = 4.0

PAIR = 2
FIELDS = 3 * PAIR
MASKS = 2 * FIELDS
MATERIAL = MASKS + PAIR
COUNT = MATERIAL + 1
EDGE = 2 * COUNT
GRAM = EDGE + 2
REACH = 4
f32 = jnp.float32
bf16 = jnp.bfloat16


def dot(a, b, contract, precision=None):
    return lax.dot_general(
        a, b, ((contract[:1], contract[1:]), ((), ())),
        precision=precision, preferred_element_type=f32,
    )


def lanes_of(shape):
    return lax.broadcasted_iota(jnp.int32, shape, len(shape) - 1)


def rows_of(shape):
    return lax.broadcasted_iota(jnp.int32, shape, len(shape) - 2)


def start_kernel(now, prev, basis, ids, mask, out, down, up, local, now_in, prev_in, basis_in, ids_in, mask_in, stage, sems):
    layers, comps, ny, nz, modes = basis.shape
    slabs = out.shape[0]
    moved = [(now, now_in), (prev, prev_in)]
    moved += [(basis.at[x, c], basis_in.at[x, c]) for x in range(layers) for c in range(comps)]
    moved += [(ids, ids_in), (mask, mask_in)]
    moved = [pltpu.make_async_copy(*pair, sems.at[k]) for k, pair in enumerate(moved)]
    for copy in moved:
        copy.start()
    moved[0].wait()
    moved[1].wait()
    modal = jnp.concatenate([now_in[...].astype(f32), prev_in[...].astype(f32)]).astype(bf16)
    gram = jnp.zeros((modes, modes), f32)
    for x in range(layers):
        for c in range(comps):
            at = x * comps + c
            moved[2 + at].wait()
            rows = basis_in[x, c].reshape(ny * nz, modes)
            both = dot(modal, rows, (1, 1))
            for y in range(ny):
                stage[at, pl.ds(y, 2 * CASES, stride=ny), :] = both[:, y * nz : (y + 1) * nz]
            for r in range(2 * CASES):
                j = r % CASES
                field = (r // CASES) * FIELDS + (j % PAIR) * comps + c
                out[j // PAIR, 2 * field + x] = stage[at, r * ny : (r + 1) * ny, :]
            gram = gram + dot(rows, rows, (0, 0))
    moved[-2].wait()
    moved[-1].wait()
    half = modes // 2
    share = half // slabs
    lane = lanes_of((half, modes))
    packed = jnp.where((lane < half) & (lane <= rows_of((half, modes))), pltpu.roll(gram[half:], half, 1), gram[:half])
    own = jnp.sum(jnp.where(rows_of(gram.shape) == lanes_of(gram.shape), gram, 0.0), axis=0, keepdims=True)
    local[...] = jnp.zeros(local.shape, f32)
    local[0:1] = pltpu.roll(own, half, 1)
    local[1:2] = own
    for p in range(slabs):
        for x in range(layers):
            for i in range(PAIR):
                out[p, 2 * (MASKS + i) + x] = mask_in[PAIR * p + i, x].astype(f32)
            out[p, 2 * MATERIAL + x] = (ids_in[x] + 1).astype(f32)
        for t in range(share // 8):
            out[p, GRAM + t] = packed[share * p + 8 * t : share * p + 8 * t + 8]
        quarter = lanes_of((ny, nz)) // REACH
        for t in range(2):
            low = jnp.zeros((ny, nz), f32)
            high = jnp.zeros((ny, nz), f32)
            for g in range(16):
                tile = 16 * t + g
                if tile < 2 * COUNT:
                    v = out[p, tile]
                    low = jnp.where(quarter == 2 * g, pltpu.roll(v, 8 * g, 1) if g else v, low)
                    turn = (8 * g + 8) % nz
                    high = jnp.where(quarter == 2 * g + 1, pltpu.roll(v, turn, 1) if turn else v, high)
            down[p, t] = low
            up[p, t] = high
            out[p, EDGE + t] = jnp.zeros((ny, nz), f32)


def faces_kernel(block, down, up):
    slabs = block.shape[0]
    first = rows_of(block.shape[2:]) < REACH
    for g in range(slabs):
        for q in range(COUNT + 1):
            a = block[g, 2 * q]
            b = pltpu.roll(block[g, 2 * q + 1], REACH, 0)
            down[g, q] = jnp.where(first, a, b)
            up[g, q] = jnp.where(first, b, a)


def steps_kernel(place, drive, moduli, block, above, below, out, share, fields, masks, stiff, weight, couple, diagonal):
    slabs, _, ny, nz = block.shape
    nx = 2 * slabs
    first = rows_of((ny, nz)) < REACH
    lane = lanes_of((ny, nz))
    zero = jnp.zeros((ny, nz), f32)
    wide_zero = jnp.zeros((2 * ny, 2 * nz), f32)
    for g in range(slabs):
        edges = [
            (block[g, EDGE], jnp.where(first, above[g, COUNT], below[g, COUNT])),
            (block[g, EDGE + 1], pltpu.roll(jnp.where(first, below[g, COUNT], above[g, COUNT]), REACH, 0)),
        ]
        for q in range(COUNT):
            beside = (
                jnp.where(first, above[g, q], below[g, q]),
                pltpu.roll(jnp.where(first, below[g, q], above[g, q]), REACH, 0),
            )
            for i in range(2):
                x = 2 * g + i
                spot = 2 * q + i
                ends = []
                for edge in edges[spot // 16]:
                    turn = 8 * (spot % 16)
                    right = pltpu.roll(edge, (nz - turn) % nz, 1) if turn else edge
                    left = pltpu.roll(edge, (2 * nz - 8 - turn) % nz, 1) if (nz - 8 - turn) % nz else edge
                    ends.append(jnp.where(lane < REACH, right, jnp.where(lane >= nz - REACH, left, zero)))
                parts = ((block[g, spot], ends[0]), (beside[i], ends[1]))
                for k in range(2):
                    for h in range(2):
                        here = (slice(k * ny, (k + 1) * ny), slice(h * nz, (h + 1) * nz))
                        value = parts[k][h]
                        if q < FIELDS:
                            fields[0, q, 1 + x, here[0], here[1]] = value
                        elif q < MASKS:
                            fields[1, q - FIELDS, 1 + x, here[0], here[1]] = value
                        elif q < MATERIAL:
                            masks[q - MASKS, x, here[0], here[1]] = value
                        else:
                            for prop in range(3):
                                level = zero
                                for m in range(moduli.shape[1]):
                                    level = jnp.where(value == m + 1.0, moduli[prop, m], level)
                                if prop < 2:
                                    stiff[prop, 1 + x, here[0], here[1]] = level
                                else:
                                    weight[x, here[0], here[1]] = step_squared * level
    for x in (0, nx + 1):
        for f in range(FIELDS):
            fields[0, f, x] = wide_zero
            fields[1, f, x] = wide_zero
        stiff[0, x] = wide_zero
        stiff[1, x] = wide_zero
    for t in range(share.shape[0]):
        total = block[0, GRAM + t]
        for g in range(1, slabs):
            total = total + block[g, GRAM + t]
        share[t] = total

    def beside_of(ref, lead, x):
        v = ref[lead + (x + 1,)]
        return v, (
            ref[lead + (x,)], ref[lead + (x + 2,)],
            pltpu.roll(v, 1, 0), pltpu.roll(v, 2 * ny - 1, 0),
            pltpu.roll(v, 1, 1), pltpu.roll(v, 2 * nz - 1, 1),
        )

    def prepare(x, carry):
        half = 0.5 * weight[x]
        sums = []
        for kind in range(2):
            v, near = beside_of(stiff, (kind,), x)
            pairs = []
            for d in range(6):
                value = half * (v + near[d])
                couple[kind, d, x] = value
                pairs.append(value)
            sums.append([pairs[2 * a] + pairs[2 * a + 1] for a in range(3)])
        for c in range(3):
            total = sums[0][c] + sums[1][(c + 1) % 3] + sums[1][(c + 2) % 3]
            diagonal[c, x] = 2.0 - total
        for i in range(PAIR):
            masks[i, x] = masks[i, x] * weight[x]
        return carry

    lax.fori_loop(0, nx, prepare, 0)
    slab = place[0]
    for s in range(STEPS):
        ramp = min(1.0, (s + 1) / ramp_steps)
        last = s == STEPS - 1
        own = (slice(0, ny), slice(0, nz)) if last else (slice(None), slice(None))

        def step(x, carry):
            for i in range(PAIR):
                for c in range(3):
                    f = 3 * i + c
                    now, to = fields.at[s % 2, f], fields.at[1 - s % 2, f]
                    v, near = beside_of(now, (), x)
                    if last:
                        v, near = v[own], [n[own] for n in near]
                    value = diagonal[(c, x) + own] * v - to[(x + 1,) + own]
                    value = value + masks[(i, x) + own] * (drive[c, PAIR * slab + i] * ramp)
                    for d in range(6):
                        kind = 0 if d // 2 == c else 1
                        value = value + couple[(kind, d, x) + own] * near[d]
                    if not last:
                        to[x + 1] = value
                    out[x // 2, s, f, x % 2] = value[:ny, :nz]
            return carry

        lax.fori_loop(0, nx, step, 0)


def project_kernel(basis, states, share, local, out, stage):
    layers, comps, ny, nz, modes = basis.shape
    count = STEPS * CASES
    coef = jnp.zeros((count, modes), f32)
    square = jnp.zeros((count, count), f32)
    for x in range(layers):
        for c in range(comps):
            at = x * comps + c
            for s in range(STEPS):
                for j in range(CASES):
                    r = s * CASES + j
                    stage[at, r * ny : (r + 1) * ny, :] = states[j // PAIR, s, (j % PAIR) * comps + c, x]
            block = jnp.concatenate(
                [stage[at, pl.ds(y, count, stride=ny), :].astype(bf16) for y in range(ny)], axis=1
            )
            coef = coef + dot(block, basis[x, c].reshape(ny * nz, modes), (1, 0))
            square = square + dot(block, block, (1, 1))
    lane = lanes_of((CASES, count))
    tile = jnp.zeros((CASES, count), f32)
    for s in range(STEPS):
        tile = jnp.where(lane // CASES == s, square[s * CASES : (s + 1) * CASES], tile)
    tile = jnp.concatenate([tile, jnp.zeros((CASES, modes - count), f32)], axis=1)
    tile = jnp.where(lanes_of(tile.shape) < modes // 2, tile, local[...])
    for g in range(out.shape[0]):
        out[g, :count] = coef
        out[g, count : count + CASES] = tile
        for t in range(share.shape[0]):
            out[g, count + CASES + 8 * t : count + CASES + 8 * t + 8] = share[t]


def sum_kernel(parts, out):
    total = parts[0]
    for g in range(1, parts.shape[0]):
        total = total + parts[g]
    for g in range(out.shape[0]):
        out[g] = total


def factor(gram):
    rows = rows_of(gram.shape)
    lane = lanes_of(gram.shape)
    work = jnp.where(lane < CASES, gram, jnp.where(lane == rows + CASES, 1.0, 0.0))
    for p in range(CASES - 1):
        ratio = work[:, p : p + 1] * (1.0 / work[p : p + 1, p : p + 1])
        work = work - jnp.where(rows > p, ratio, 0.0) * work[p : p + 1]
    pivots = jnp.sum(jnp.where(lane == rows, work, 0.0), axis=1, keepdims=True)
    work = work * (1.0 / jnp.sqrt(pivots))
    upper = jnp.where((rows <= lane) & (lane < CASES), work, 0.0)
    inverse = jnp.where(lane < CASES, pltpu.roll(work, gram.shape[1] - CASES, 1), 0.0)
    return upper, inverse


def mixed(small, rows):
    total = small[:, :1] * rows[:1]
    for i in range(1, CASES):
        total = total + small[:, i : i + 1] * rows[i : i + 1]
    return total


def padded(rows):
    return jnp.concatenate([rows, jnp.zeros((rows.shape[1] - rows.shape[0], rows.shape[1]), f32)])


def pieces_of(value):
    pieces = []
    for _ in range(3):
        piece = value.astype(bf16)
        pieces.append(piece)
        value = value - piece.astype(f32)
    return pieces


def exact(rounded, pieces, contract):
    total = dot(rounded, pieces[2], contract)
    return total + dot(rounded, pieces[1], contract) + dot(rounded, pieces[0], contract)


def finish_kernel(weight, parts, basis, states, displacement, modes_out, coefficients, factors, stage, held, sems):
    layers, comps, ny, nz, modes = basis.shape
    moved = []
    for c in range(comps):
        for j in range(CASES):
            moved.append(pltpu.make_async_copy(
                states.at[j // PAIR, STEPS - 1, (j % PAIR) * comps + c], displacement.at[c, j], sems.at[len(moved)]
            ))
            moved[-1].start()
    count = STEPS * CASES
    half = modes // 2
    high = lax.Precision.HIGHEST
    own = parts[0, : count + CASES]
    for g in range(1, parts.shape[0]):
        own = own + parts[g, : count + CASES]
    own = own * weight
    coef, square = own[:count], own[count:]
    packed = jnp.concatenate([parts[g, count + CASES :] for g in range(parts.shape[0])]) * weight
    lane, row = lanes_of(packed.shape), rows_of(packed.shape)
    flipped = padded(packed).T
    diagonal = jnp.where(lane[:1] < half, pltpu.roll(square[:1], half, 1), square[1:2])
    top = jnp.where(lane < row, flipped[:half], packed)
    top = jnp.where(lane == row, diagonal, top)
    bottom = jnp.where(lane - half <= row, pltpu.roll(packed, half, 1), pltpu.roll(flipped[:half], half, 1))
    bottom = jnp.where(lane < half, flipped[half:], bottom)
    bottom = jnp.where(lane - half == row, diagonal, bottom)
    gram = pieces_of(jnp.concatenate([top, bottom]))
    lane = lanes_of(square.shape)

    def block_of(rows, s):
        turn = (modes - s * CASES) % modes
        rows = pltpu.roll(rows, turn, 1) if turn else rows
        return jnp.where(lane < CASES, rows, 0.0)

    def change_of(coef):
        rounded = coef.astype(bf16)
        left = coef - exact(rounded, gram, (1, 0))
        wide = padded(rounded.astype(f32)).astype(bf16)
        change = exact(rounded, pieces_of(padded(left)), (1, 1))
        for piece in pieces_of(coef)[::-1]:
            change = change + dot(piece, wide, (1, 1))
        return rounded.astype(f32), left, change

    rounded, left, change = change_of(coef)
    first, second = [], []
    for s in range(STEPS):
        at = slice(s * CASES, (s + 1) * CASES)
        first.append(factor(block_of(square - change[at], s)))
        second.append(mixed(first[s][1], left[at]))
    second = jnp.concatenate(second)
    rounded_2, left_2, change = change_of(second)
    for s in range(STEPS):
        at = slice(s * CASES, (s + 1) * CASES)
        whole = dot(first[s][0], padded(first[s][1]), (1, 1), high)
        upper, inverse = factor(whole - block_of(change[at], s))
        factors[s] = mixed(upper, first[s][0])[:, :CASES]
        coefficients[s, 0] = coef[at]
        coefficients[s, 1] = second[at]
    mix = mixed(inverse, first[-1][1])
    shift = mixed(mix, rounded[at]) + mixed(inverse, rounded_2[at])
    pieces = jnp.concatenate([piece.astype(f32) for piece in pieces_of(shift)]).astype(bf16)
    scalars = [[mix[i : i + 1, j : j + 1] for j in range(CASES)] for i in range(CASES)]
    for c in range(comps):
        for x in range(layers):
            at = x * comps + c
            taken = dot(pieces, basis[x, c].reshape(ny * nz, modes), (1, 1))
            taken = taken[:CASES] + taken[CASES : 2 * CASES] + taken[2 * CASES :]
            for y in range(ny):
                stage[at, pl.ds(y, CASES, stride=ny), :] = taken[:, y * nz : (y + 1) * nz]
            snapshot = [
                states[j // PAIR, STEPS - 1, (j % PAIR) * comps + c, x].astype(bf16).astype(f32) for j in range(CASES)
            ]
            for i in range(CASES):
                total = scalars[i][0] * snapshot[0]
                for j in range(1, CASES):
                    total = total + scalars[i][j] * snapshot[j]
                held[c, i, x] = total - stage[at, i * ny : (i + 1) * ny, :]
        moved.append(pltpu.make_async_copy(held.at[c], modes_out.at[c], sems.at[len(moved)]))
        moved[-1].start()
    for copy in moved:
        copy.wait()


def call(kernel, outs, inputs, scratch=(), scalars=0, copies=0, ins_away=0, outs_away=0, room=40):
    vmem = pl.BlockSpec(memory_space=pltpu.VMEM)
    smem = pl.BlockSpec(memory_space=pltpu.SMEM)
    away = pl.BlockSpec(memory_space=pltpu.HBM)
    scratch = [pltpu.VMEM(shape, f32) if isinstance(shape, tuple) else shape for shape in scratch]
    return pl.pallas_call(
        kernel,
        out_shape=[jax.ShapeDtypeStruct(shape, f32) for shape in outs],
        in_specs=[smem] * scalars + [away] * ins_away + [vmem] * (len(inputs) - scalars - ins_away),
        out_specs=[away] * outs_away + [vmem] * (len(outs) - outs_away),
        scratch_shapes=scratch + ([pltpu.SemaphoreType.DMA((copies,))] if copies else []),
        compiler_params=pltpu.CompilerParams(vmem_limit_bytes=room << 20),
    )(*inputs)


def sent(block, axis, forward):
    count = lax.axis_size(axis)
    pairs = [(i, i + 1) for i in range(count - 1)]
    return lax.ppermute(block, axis, pairs if forward else [(b, a) for a, b in pairs])


def turned(parts, axis):
    return lax.all_to_all(parts, axis, 0, 0, tiled=True)


def shards(basis, modal_now, modal_prev, material_ids, moduli, drive_mask, drive):
    layers, comps, ny, nz, modes = basis.shape
    slabs, rows, depth = (lax.axis_size(a) for a in ("gx", "gy", "gz"))
    dof_weight = 1.0 / (3.0 * layers * ny * nz * slabs * rows * depth)
    tile = (ny, nz)
    share = modes // 2 // slabs // 8
    blocks = layers * comps
    inputs = [pltpu.with_memory_space_constraint(a, pltpu.HBM) for a in (modal_now.T, modal_prev.T, basis, material_ids, drive_mask)]
    block, down, up, local = call(
        start_kernel,
        [(slabs, GRAM + share) + tile, (slabs, 2) + tile, (slabs, 2) + tile, (CASES, modes)],
        inputs,
        [pltpu.VMEM(a.shape, a.dtype) for a in inputs] + [(blocks, 2 * CASES * ny, nz)],
        copies=blocks + 4,
        ins_away=5,
    )
    edge = sent(down, "gz", False) + sent(up, "gz", True)
    block = turned(lax.dynamic_update_slice(block, edge, (0, EDGE, 0, 0)), "gx")
    down, up = call(faces_kernel, [(slabs, COUNT + 1) + tile] * 2, [block])
    above, below = sent(down, "gy", False), sent(up, "gy", True)
    nx = layers * slabs
    wide = (2 * ny, 2 * nz)
    place = lax.axis_index("gx").astype(jnp.int32)[None]
    states, gram = call(
        steps_kernel,
        [(slabs, STEPS, FIELDS, layers) + tile, (share,) + tile],
        [place, drive, moduli, block, above, below],
        [
            (2, FIELDS, nx + 2) + wide, (PAIR, nx) + wide, (2, nx + 2) + wide, (nx,) + wide,
            (2, 6, nx) + wide, (3, nx) + wide,
        ],
        3,
    )
    states = turned(states, "gx")
    count = STEPS * CASES
    width = count + CASES + 8 * share
    parts, = call(
        project_kernel, [(rows, width, modes)], [basis, states, gram, local], [(blocks, count * ny, nz)]
    )
    parts, = call(sum_kernel, [(depth, width, modes)], [turned(parts, "gy")])
    parts, = call(sum_kernel, [(slabs, width, modes)], [turned(parts, "gz")])
    held = (comps, CASES, layers) + tile
    displacement, modes_out, coefficients, factors = call(
        lambda *refs: finish_kernel(dof_weight, *refs),
        [held, held, (STEPS, 2, CASES, modes), (STEPS, CASES, CASES)],
        [turned(parts, "gx"), basis, states],
        [(blocks, CASES * ny, nz), held],
        copies=comps * CASES + comps,
        outs_away=2,
    )
    return displacement, modes_out, coefficients.transpose(0, 1, 3, 2), factors


def solution(mesh):
    in_specs = (
        P("gx", None, "gy", "gz", None),
        P(),
        P(),
        P("gx", "gy", "gz"),
        P(),
        P(None, "gx", "gy", "gz"),
        P(),
    )
    out_specs = (P(None, None, "gx", "gy", "gz"), P(None, None, "gx", "gy", "gz"), P(), P())
    return jax.shard_map(
        shards, mesh=mesh, in_specs=in_specs, out_specs=out_specs, check_vma=False
    )
```

```python
import jax
import jax.numpy as jnp
from jax import lax
from jax.experimental import pallas as pl
from jax.experimental.pallas import tpu as pltpu
from jax.sharding import PartitionSpec as P

STEPS = 4
CASES = 8
step_squared = 0.1
ramp_steps = 4.0

PAIR = 2
FIELDS = 3 * PAIR
MASKS = 2 * FIELDS
MATERIAL = MASKS + PAIR
COUNT = MATERIAL + 1
EDGE = 2 * COUNT
GRAM = EDGE + 2
REACH = 4
f32 = jnp.float32
bf16 = jnp.bfloat16


def dot(a, b, contract, precision=None):
    return lax.dot_general(
        a, b, ((contract[:1], contract[1:]), ((), ())),
        precision=precision, preferred_element_type=f32,
    )


def lanes_of(shape):
    return lax.broadcasted_iota(jnp.int32, shape, len(shape) - 1)


def rows_of(shape):
    return lax.broadcasted_iota(jnp.int32, shape, len(shape) - 2)


def start_kernel(now, prev, basis, ids, mask, out, down, up, now_in, prev_in, basis_in, ids_in, mask_in, stage, sems):
    layers, comps, ny, nz, modes = basis.shape
    slabs = out.shape[0]
    moved = [(now, now_in), (prev, prev_in)]
    moved += [(basis.at[x, c], basis_in.at[x, c]) for x in range(layers) for c in range(comps)]
    moved += [(ids, ids_in), (mask, mask_in)]
    moved = [pltpu.make_async_copy(*pair, sems.at[k]) for k, pair in enumerate(moved)]
    for copy in moved:
        copy.start()
    moved[0].wait()
    moved[1].wait()
    modal = jnp.concatenate([now_in[...].astype(f32), prev_in[...].astype(f32)]).astype(bf16)
    for x in range(layers):
        for c in range(comps):
            at = x * comps + c
            moved[2 + at].wait()
            rows = basis_in[x, c].reshape(ny * nz, modes)
            both = dot(modal, rows, (1, 1))
            for y in range(ny):
                stage[at, pl.ds(y, 2 * CASES, stride=ny), :] = both[:, y * nz : (y + 1) * nz]
            for r in range(2 * CASES):
                j = r % CASES
                field = (r // CASES) * FIELDS + (j % PAIR) * comps + c
                out[j // PAIR, 2 * field + x] = stage[at, r * ny : (r + 1) * ny, :]
    moved[-2].wait()
    moved[-1].wait()
    for p in range(slabs):
        for x in range(layers):
            for i in range(PAIR):
                out[p, 2 * (MASKS + i) + x] = mask_in[PAIR * p + i, x].astype(f32)
            out[p, 2 * MATERIAL + x] = (ids_in[x] + 1).astype(f32)
        quarter = lanes_of((ny, nz)) // REACH
        for t in range(2):
            low = jnp.zeros((ny, nz), f32)
            high = jnp.zeros((ny, nz), f32)
            for g in range(16):
                tile = 16 * t + g
                if tile < 2 * COUNT:
                    v = out[p, tile]
                    low = jnp.where(quarter == 2 * g, pltpu.roll(v, 8 * g, 1) if g else v, low)
                    turn = (8 * g + 8) % nz
                    high = jnp.where(quarter == 2 * g + 1, pltpu.roll(v, turn, 1) if turn else v, high)
            down[p, t] = low
            up[p, t] = high
        for t in range(EDGE, out.shape[1]):
            out[p, t] = jnp.zeros((ny, nz), f32)


def gram_kernel(basis, out, local):
    layers, comps, ny, nz, modes = basis.shape
    slabs = out.shape[0]
    gram = jnp.zeros((modes, modes), f32)
    for x in range(layers):
        for c in range(comps):
            rows = basis[x, c].reshape(ny * nz, modes)
            gram = gram + dot(rows, rows, (0, 0))
    half = modes // 2
    share = half // slabs
    lane = lanes_of((half, modes))
    packed = jnp.where((lane < half) & (lane <= rows_of((half, modes))), pltpu.roll(gram[half:], half, 1), gram[:half])
    own = jnp.sum(jnp.where(rows_of(gram.shape) == lanes_of(gram.shape), gram, 0.0), axis=0, keepdims=True)
    local[...] = jnp.zeros(local.shape, f32)
    local[0:1] = pltpu.roll(own, half, 1)
    local[1:2] = own
    for p in range(slabs):
        for t in range(share // 8):
            out[p, t] = packed[share * p + 8 * t : share * p + 8 * t + 8]


def faces_kernel(block, down, up):
    slabs = block.shape[0]
    first = rows_of(block.shape[2:]) < REACH
    for g in range(slabs):
        for q in range(COUNT + 1):
            a = block[g, 2 * q]
            b = pltpu.roll(block[g, 2 * q + 1], REACH, 0)
            down[g, q] = jnp.where(first, a, b)
            up[g, q] = jnp.where(first, b, a)


def steps_kernel(
    place, drive, moduli, block, above, below, out, share, fields, masks, stiff, weight, couple, diagonal,
    side, side_mask, side_stiff, side_couple, side_diagonal,
):
    slabs, _, ny, nz = block.shape
    nx = 2 * slabs
    first = rows_of((ny, nz)) < REACH
    zero = jnp.zeros((ny, nz), f32)
    plane_zero = jnp.zeros((2 * ny, nz), f32)
    halves = (slice(0, ny), slice(ny, 2 * ny))

    def level_of(value, prop):
        level = zero
        for m in range(moduli.shape[1]):
            level = jnp.where(value == m + 1.0, moduli[prop, m], level)
        return level

    group = lanes_of((ny, nz)) // 16
    sides = {}
    for g in range(slabs):
        edges = [
            (block[g, EDGE], jnp.where(first, above[g, COUNT], below[g, COUNT])),
            (block[g, EDGE + 1], pltpu.roll(jnp.where(first, below[g, COUNT], above[g, COUNT]), REACH, 0)),
        ]
        for q in range(COUNT):
            beside = (
                jnp.where(first, above[g, q], below[g, q]),
                pltpu.roll(jnp.where(first, below[g, q], above[g, q]), REACH, 0),
            )
            for i in range(2):
                x = 2 * g + i
                for rows, value in zip(halves, (block[g, 2 * q + i], beside[i])):
                    if q < FIELDS:
                        fields[0, q, 1 + x, rows] = value
                    elif q < MASKS:
                        fields[1, q - FIELDS, 1 + x, rows] = value
                    elif q < MATERIAL:
                        masks[q - MASKS, x, rows] = value
                    else:
                        stiff[0, 1 + x, rows] = level_of(value, 0)
                        stiff[1, 1 + x, rows] = level_of(value, 1)
                        weight[x, rows] = step_squared * level_of(value, 2)
            if q < MASKS:
                key, cases = (q // FIELDS, q % 3), (q % FIELDS // 3,)
            elif q < MATERIAL:
                key, cases = "mask", (q - MASKS,)
            else:
                key, cases = "material", (0, 1)
            for k in range(2):
                for i in cases:
                    turn = (64 * i + 16 * g - 16 * (q % 8)) % nz
                    edge = edges[q // 8][k]
                    edge = pltpu.roll(edge, turn, 1) if turn else edge
                    sides[key, k] = jnp.where(group == 4 * i + g, edge, sides.get((key, k), zero))
    side_weight = []
    for k, rows in enumerate(halves):
        for t in range(2):
            for c in range(3):
                side[t, c, rows] = sides[(t, c), k]
        side_stiff[0, rows] = level_of(sides["material", k], 0)
        side_stiff[1, rows] = level_of(sides["material", k], 1)
        heavy = step_squared * level_of(sides["material", k], 2)
        side_weight.append(heavy)
        side_mask[rows] = sides["mask", k] * heavy
    for x in (0, nx + 1):
        for f in range(FIELDS):
            fields[0, f, x] = plane_zero
            fields[1, f, x] = plane_zero
        stiff[0, x] = plane_zero
        stiff[1, x] = plane_zero
    for t in range(share.shape[0]):
        total = block[0, GRAM + t]
        for g in range(1, slabs):
            total = total + block[g, GRAM + t]
        share[t] = total

    lane = lanes_of((2 * ny, nz))
    spot = lane % 8
    layer = lane % 64 // 8

    def turned_by(v, shift):
        return pltpu.roll(v, shift % nz, 1) if shift % nz else v

    def near_main(get, edge, base, x, rows):
        v = get(x + 1)
        part = lambda a: a[:rows]
        lanes = lane[:rows]
        low = jnp.where(lanes == 0, turned_by(edge[:rows], -(base + 7)), pltpu.roll(part(v), 1, 1))
        high = jnp.where(lanes == nz - 1, turned_by(edge[:rows], nz - 1 - base), pltpu.roll(part(v), nz - 1, 1))
        return part(v), (
            part(get(x)), part(get(x + 2)), part(pltpu.roll(v, 1, 0)), part(pltpu.roll(v, 2 * ny - 1, 0)), low, high
        )

    def near_side(v, gets):
        low, high = plane_zero, plane_zero
        for i in range(PAIR):
            for x in range(nx):
                base = 64 * i + 8 * x
                main = gets[i](x + 1)
                low = jnp.where(lane == base, turned_by(main, base + 1), low)
                high = jnp.where(lane == base + 7, turned_by(main, base + 7), high)
        return (
            jnp.where(layer == 0, 0.0, pltpu.roll(v, 8, 1)), jnp.where(layer == nx - 1, 0.0, pltpu.roll(v, nz - 8, 1)),
            pltpu.roll(v, 1, 0), pltpu.roll(v, 2 * ny - 1, 0),
            jnp.where(spot == 0, low, pltpu.roll(v, 1, 1)), jnp.where(spot == 7, high, pltpu.roll(v, nz - 1, 1)),
        )

    def coupled(half, kinds, store, store_diagonal):
        sums = []
        for kind in range(2):
            v, near = kinds[kind]
            pairs = []
            for d in range(6):
                value = half * (v + near[d])
                store(kind, d, value)
                pairs.append(value)
            sums.append([pairs[2 * a] + pairs[2 * a + 1] for a in range(3)])
        for c in range(3):
            store_diagonal(c, 2.0 - (sums[0][c] + sums[1][(c + 1) % 3] + sums[1][(c + 2) % 3]))

    def setter(ref, *tail):
        def put(*at):
            ref[at[:-1] + tail] = at[-1]
        return put

    for x in range(nx):
        kinds = [near_main(lambda at: stiff[kind, at], side_stiff[kind], 8 * x, x, 2 * ny) for kind in range(2)]
        coupled(0.5 * weight[x], kinds, setter(couple, x), setter(diagonal, x))
        for i in range(PAIR):
            masks[i, x] = masks[i, x] * weight[x]
    kinds = [(side_stiff[k], near_side(side_stiff[k], [lambda at: stiff[k, at]] * PAIR)) for k in range(2)]
    coupled(0.5 * jnp.concatenate(side_weight), kinds, setter(side_couple), setter(side_diagonal))

    slab = place[0]

    def advanced(v, near, before, centre, forced, pairs, c):
        value = centre * v - before + forced
        for d in range(6):
            value = value + pairs(0 if d // 2 == c else 1, d) * near[d]
        return value

    for s in range(STEPS):
        ramp = min(1.0, (s + 1) / ramp_steps)
        last = s == STEPS - 1
        rows = ny if last else 2 * ny
        now, to = s % 2, 1 - s % 2
        force = [[drive[c, PAIR * slab + i] * ramp for c in range(3)] for i in range(PAIR)]
        for c in range(3):
            gets = [lambda at, f=3 * i + c: fields[now, f, at] for i in range(PAIR)]
            edge = side[now, c]
            if not last:
                push = jnp.where(lane < 64, force[0][c], force[1][c])
                side[to, c] = advanced(
                    edge, near_side(edge, gets), side[to, c], side_diagonal[c], side_mask[...] * push,
                    lambda kind, d: side_couple[kind, d], c,
                )
            for x in range(nx):
                for i in range(PAIR):
                    f = 3 * i + c
                    v, near = near_main(gets[i], edge, 64 * i + 8 * x, x, rows)
                    value = advanced(
                        v, near, fields[to, f, x + 1, :rows], diagonal[c, x, :rows], masks[i, x, :rows] * force[i][c],
                        lambda kind, d: couple[kind, d, x, :rows], c,
                    )
                    if not last:
                        fields[to, f, x + 1] = value
                    out[x // 2, s, f, x % 2] = value[:ny]


def project_kernel(basis, states, share, local, out, stage):
    layers, comps, ny, nz, modes = basis.shape
    count = STEPS * CASES
    coef = jnp.zeros((count, modes), f32)
    square = jnp.zeros((count, count), f32)
    for x in range(layers):
        for c in range(comps):
            at = x * comps + c
            for s in range(STEPS):
                for j in range(CASES):
                    r = s * CASES + j
                    stage[at, r * ny : (r + 1) * ny, :] = states[j // PAIR, s, (j % PAIR) * comps + c, x]
            block = jnp.concatenate(
                [stage[at, pl.ds(y, count, stride=ny), :].astype(bf16) for y in range(ny)], axis=1
            )
            coef = coef + dot(block, basis[x, c].reshape(ny * nz, modes), (1, 0))
            square = square + dot(block, block, (1, 1))
    lane = lanes_of((CASES, count))
    tile = jnp.zeros((CASES, count), f32)
    for s in range(STEPS):
        tile = jnp.where(lane // CASES == s, square[s * CASES : (s + 1) * CASES], tile)
    tile = jnp.concatenate([tile, jnp.zeros((CASES, modes - count), f32)], axis=1)
    tile = jnp.where(lanes_of(tile.shape) < modes // 2, tile, local[...])
    half = count // 2
    for g in range(out.shape[0]):
        h = g % 2
        out[g, :half] = coef[h * half : (h + 1) * half]
        out[g, half : half + CASES] = tile
        out[g, half + CASES :] = share[h]


def sum_kernel(parts, out):
    total = parts[0]
    for g in range(1, parts.shape[0]):
        total = total + parts[g]
    for g in range(out.shape[0]):
        out[g] = total


def factor(gram):
    rows = rows_of(gram.shape)
    lane = lanes_of(gram.shape)
    work = jnp.where(lane < CASES, gram, jnp.where(lane == rows + CASES, 1.0, 0.0))
    for p in range(CASES - 1):
        ratio = work[:, p : p + 1] * (1.0 / work[p : p + 1, p : p + 1])
        work = work - jnp.where(rows > p, ratio, 0.0) * work[p : p + 1]
    pivots = jnp.sum(jnp.where(lane == rows, work, 0.0), axis=1, keepdims=True)
    work = work * (1.0 / jnp.sqrt(pivots))
    upper = jnp.where((rows <= lane) & (lane < CASES), work, 0.0)
    inverse = jnp.where(lane < CASES, pltpu.roll(work, gram.shape[1] - CASES, 1), 0.0)
    return upper, inverse


def mixed(small, rows):
    total = small[:, :1] * rows[:1]
    for i in range(1, CASES):
        total = total + small[:, i : i + 1] * rows[i : i + 1]
    return total


def padded(rows):
    return jnp.concatenate([rows, jnp.zeros((rows.shape[1] - rows.shape[0], rows.shape[1]), f32)])


def pieces_of(value):
    pieces = []
    for _ in range(3):
        piece = value.astype(bf16)
        pieces.append(piece)
        value = value - piece.astype(f32)
    return pieces


def exact(rounded, pieces, contract):
    total = dot(rounded, pieces[2], contract)
    return total + dot(rounded, pieces[1], contract) + dot(rounded, pieces[0], contract)


def finish_kernel(weight, parts, basis, states, displacement, modes_out, coefficients, factors, stage, held, sems):
    layers, comps, ny, nz, modes = basis.shape
    moved = []
    for c in range(comps):
        for j in range(CASES):
            moved.append(pltpu.make_async_copy(
                states.at[j // PAIR, STEPS - 1, (j % PAIR) * comps + c], displacement.at[c, j], sems.at[len(moved)]
            ))
            moved[-1].start()
    count = STEPS * CASES
    half = modes // 2
    high = lax.Precision.HIGHEST
    members, upto = parts.shape[0], count // 2 + CASES
    owns = []
    for h in range(2):
        own = parts[h, :upto]
        for g in range(h + 2, members, 2):
            own = own + parts[g, :upto]
        owns.append(own * weight)
    coef = jnp.concatenate([own[: count // 2] for own in owns])
    square = owns[0][count // 2 :]
    packed = jnp.concatenate([parts[g, upto:] for g in range(members)]) * weight
    lane, row = lanes_of(packed.shape), rows_of(packed.shape)
    flipped = padded(packed).T
    diagonal = jnp.where(lane[:1] < half, pltpu.roll(square[:1], half, 1), square[1:2])
    top = jnp.where(lane < row, flipped[:half], packed)
    top = jnp.where(lane == row, diagonal, top)
    bottom = jnp.where(lane - half <= row, pltpu.roll(packed, half, 1), pltpu.roll(flipped[:half], half, 1))
    bottom = jnp.where(lane < half, flipped[half:], bottom)
    bottom = jnp.where(lane - half == row, diagonal, bottom)
    gram = pieces_of(jnp.concatenate([top, bottom]))
    lane = lanes_of(square.shape)

    def block_of(rows, s):
        turn = (modes - s * CASES) % modes
        rows = pltpu.roll(rows, turn, 1) if turn else rows
        return jnp.where(lane < CASES, rows, 0.0)

    def change_of(coef):
        rounded = coef.astype(bf16)
        left = coef - exact(rounded, gram, (1, 0))
        wide = padded(rounded.astype(f32)).astype(bf16)
        change = exact(rounded, pieces_of(padded(left)), (1, 1))
        for piece in pieces_of(coef)[::-1]:
            change = change + dot(piece, wide, (1, 1))
        return rounded.astype(f32), left, change

    def expanded(rounded, slot):
        for c in range(comps):
            for x in range(layers):
                at = x * comps + c
                taken = dot(rounded.astype(bf16), basis[x, c].reshape(ny * nz, modes), (1, 1))
                for y in range(ny):
                    stage[slot, at, pl.ds(y, CASES, stride=ny), :] = taken[:, y * nz : (y + 1) * nz]

    rounded, left, change = change_of(coef)
    expanded(rounded[count - CASES :], 0)
    first, second = [], []
    for s in range(STEPS):
        at = slice(s * CASES, (s + 1) * CASES)
        first.append(factor(block_of(square - change[at], s)))
        second.append(mixed(first[s][1], left[at]))
    second = jnp.concatenate(second)
    rounded_2, left_2, change = change_of(second)
    expanded(rounded_2[count - CASES :], 1)
    for s in range(STEPS):
        at = slice(s * CASES, (s + 1) * CASES)
        whole = dot(first[s][0], padded(first[s][1]), (1, 1), high)
        upper, inverse = factor(whole - block_of(change[at], s))
        factors[s] = mixed(upper, first[s][0])[:, :CASES]
        coefficients[s, 0] = coef[at]
        coefficients[s, 1] = second[at]
    mix = mixed(inverse, first[-1][1])
    wide = lambda small: [
        [jnp.broadcast_to(small[i : i + 1, j : j + 1], (ny, nz)) for j in range(i + 1)] for i in range(CASES)
    ]
    mix, inverse = wide(mix), wide(inverse)
    for c in range(comps):
        for x in range(layers):
            at = x * comps + c
            resid, extra = [], []
            for j in range(CASES):
                here = slice(j * ny, (j + 1) * ny)
                snapshot = states[j // PAIR, STEPS - 1, (j % PAIR) * comps + c, x].astype(bf16).astype(f32)
                resid.append(snapshot - stage[0, at, here])
                extra.append(stage[1, at, here])
            for i in range(CASES):
                total = mix[i][0] * resid[0] - inverse[i][0] * extra[0]
                for j in range(1, i + 1):
                    total = total + (mix[i][j] * resid[j] - inverse[i][j] * extra[j])
                held[c, i, x] = total
        moved.append(pltpu.make_async_copy(held.at[c], modes_out.at[c], sems.at[len(moved)]))
        moved[-1].start()
    for copy in moved:
        copy.wait()


def call(kernel, outs, inputs, scratch=(), scalars=0, copies=0, ins_away=0, outs_away=0, room=40):
    vmem = pl.BlockSpec(memory_space=pltpu.VMEM)
    smem = pl.BlockSpec(memory_space=pltpu.SMEM)
    away = pl.BlockSpec(memory_space=pltpu.HBM)
    scratch = [pltpu.VMEM(shape, f32) if isinstance(shape, tuple) else shape for shape in scratch]
    return pl.pallas_call(
        kernel,
        out_shape=[jax.ShapeDtypeStruct(shape, f32) for shape in outs],
        in_specs=[smem] * scalars + [away] * ins_away + [vmem] * (len(inputs) - scalars - ins_away),
        out_specs=[away] * outs_away + [vmem] * (len(outs) - outs_away),
        scratch_shapes=scratch + ([pltpu.SemaphoreType.DMA((copies,))] if copies else []),
        compiler_params=pltpu.CompilerParams(vmem_limit_bytes=room << 20),
    )(*inputs)


def sent(block, axis, forward):
    count = lax.axis_size(axis)
    pairs = [(i, i + 1) for i in range(count - 1)]
    return lax.ppermute(block, axis, pairs if forward else [(b, a) for a, b in pairs])


def turned(parts, axis):
    return lax.all_to_all(parts, axis, 0, 0, tiled=True)


def shards(basis, modal_now, modal_prev, material_ids, moduli, drive_mask, drive):
    layers, comps, ny, nz, modes = basis.shape
    slabs, rows, depth = (lax.axis_size(a) for a in ("gx", "gy", "gz"))
    dof_weight = 1.0 / (3.0 * layers * ny * nz * slabs * rows * depth)
    tile = (ny, nz)
    share = modes // 2 // slabs // 8
    blocks = layers * comps
    inputs = [pltpu.with_memory_space_constraint(a, pltpu.HBM) for a in (modal_now.T, modal_prev.T, basis, material_ids, drive_mask)]
    block, down, up = call(
        start_kernel,
        [(slabs, GRAM + share) + tile, (slabs, 2) + tile, (slabs, 2) + tile],
        inputs,
        [pltpu.VMEM(a.shape, a.dtype) for a in inputs] + [(blocks, 2 * CASES * ny, nz)],
        copies=blocks + 4,
        ins_away=5,
    )
    edge = sent(down, "gz", False) + sent(up, "gz", True)
    gram, local = call(gram_kernel, [(slabs, share) + tile, (CASES, modes)], [basis])
    block = lax.dynamic_update_slice(block, jnp.concatenate([edge, gram], axis=1), (0, EDGE, 0, 0))
    block = turned(block, "gx")
    down, up = call(faces_kernel, [(slabs, COUNT + 1) + tile] * 2, [block])
    above, below = sent(down, "gy", False), sent(up, "gy", True)
    nx = layers * slabs
    wide = (2 * ny, nz)
    place = lax.axis_index("gx").astype(jnp.int32)[None]
    states, gram = call(
        steps_kernel,
        [(slabs, STEPS, FIELDS, layers) + tile, (share,) + tile],
        [place, drive, moduli, block, above, below],
        [
            (2, FIELDS, nx + 2) + wide, (PAIR, nx) + wide, (2, nx + 2) + wide, (nx,) + wide,
            (2, 6, nx) + wide, (3, nx) + wide, (2, 3) + wide, wide, (2,) + wide, (2, 6) + wide, (3,) + wide,
        ],
        3,
    )
    states = turned(states, "gx")
    count = STEPS * CASES
    width = count // 2 + CASES + 8
    parts, = call(
        project_kernel, [(rows, width, modes)], [basis, states, gram, local], [(blocks, count * ny, nz)]
    )
    parts, = call(sum_kernel, [(depth, width, modes)], [turned(parts, "gy")])
    parts, = call(sum_kernel, [(2 * slabs, width, modes)], [turned(parts, "gz")])
    groups = [
        [(a * rows + 2 * h + core) * depth + z for a in range(slabs) for core in range(2)]
        for h in range(rows // 2)
        for z in range(depth)
    ]
    parts = lax.all_to_all(parts, ("gx", "gy", "gz"), 0, 0, tiled=True, axis_index_groups=groups)
    held = (comps, CASES, layers) + tile
    displacement, modes_out, coefficients, factors = call(
        lambda *refs: finish_kernel(dof_weight, *refs),
        [held, held, (STEPS, 2, CASES, modes), (STEPS, CASES, CASES)],
        [parts, basis, states],
        [(2, blocks, CASES * ny, nz), held],
        copies=comps * CASES + comps,
        outs_away=2,
    )
    return displacement, modes_out, coefficients.transpose(0, 1, 3, 2), factors


def solution(mesh):
    in_specs = (
        P("gx", None, "gy", "gz", None),
        P(),
        P(),
        P("gx", "gy", "gz"),
        P(),
        P(None, "gx", "gy", "gz"),
        P(),
    )
    out_specs = (P(None, None, "gx", "gy", "gz"), P(None, None, "gx", "gy", "gz"), P(), P())
    return jax.shard_map(
        shards, mesh=mesh, in_specs=in_specs, out_specs=out_specs, check_vma=False
    )
```

```python
import jax
import jax.numpy as jnp
from jax import lax
from jax.experimental import pallas as pl
from jax.experimental.pallas import tpu as pltpu
from jax.sharding import PartitionSpec as P

STEPS = 4
CASES = 8
step_squared = 0.1
ramp_steps = 4.0

PAIR = 2
FIELDS = 3 * PAIR
MASKS = 2 * FIELDS
MATERIAL = MASKS + PAIR
COUNT = MATERIAL + 1
EDGE = 2 * COUNT
GRAM = EDGE + 2
REACH = 4
f32 = jnp.float32
bf16 = jnp.bfloat16


def dot(a, b, contract, precision=None):
    return lax.dot_general(
        a, b, ((contract[:1], contract[1:]), ((), ())),
        precision=precision, preferred_element_type=f32,
    )


def lanes_of(shape):
    return lax.broadcasted_iota(jnp.int32, shape, len(shape) - 1)


def rows_of(shape):
    return lax.broadcasted_iota(jnp.int32, shape, len(shape) - 2)


def start_kernel(place, odd, turn_z, now, prev, basis, ids, mask, out, even_pairs, odd_pairs, basis_in, now_in, prev_in, ids_in, mask_in, stage, sems):
    layers, comps, ny, nz, modes = basis.shape
    slabs = out.shape[0]
    moved = [(now, now_in), (prev, prev_in)]
    moved += [(basis.at[x, c], basis_in.at[x, c]) for x in range(layers) for c in range(comps)]
    moved += [(ids, ids_in), (mask, mask_in)]
    moved = [pltpu.make_async_copy(*pair, sems.at[k]) for k, pair in enumerate(moved)]
    for copy in moved:
        copy.start()
    moved[0].wait()
    moved[1].wait()
    modal = jnp.concatenate([now_in[...].astype(f32), prev_in[...].astype(f32)]).astype(bf16)
    for x in range(layers):
        for c in range(comps):
            at = x * comps + c
            moved[2 + at].wait()
            rows = basis_in[x, c].reshape(ny * nz, modes)
            both = dot(modal, rows, (1, 1))
            for y in range(ny):
                stage[at, pl.ds(y, 2 * CASES, stride=ny), :] = both[:, y * nz : (y + 1) * nz]
            for r in range(2 * CASES):
                j = r % CASES
                field = (r // CASES) * FIELDS + (j % PAIR) * comps + c
                out[j // PAIR, 2 * field + x] = stage[at, r * ny : (r + 1) * ny, :]
    moved[-2].wait()
    moved[-1].wait()
    for p in range(slabs):
        for x in range(layers):
            for i in range(PAIR):
                out[p, 2 * (MASKS + i) + x] = mask_in[PAIR * p + i, x].astype(f32)
            out[p, 2 * MATERIAL + x] = (ids_in[x] + 1).astype(f32)
        quarter = lanes_of((ny, nz)) // REACH
        upper = jnp.full((ny, nz), turn_z[0], jnp.int32) == 1
        for t in range(2):
            low = jnp.zeros((ny, nz), f32)
            high = jnp.zeros((ny, nz), f32)
            for g in range(16):
                tile = 16 * t + g
                if tile < 2 * COUNT:
                    v = out[p, tile]
                    low = jnp.where(quarter == 2 * g, pltpu.roll(v, 8 * g, 1) if g else v, low)
                    turn = (8 * g + 8) % nz
                    high = jnp.where(quarter == 2 * g + 1, pltpu.roll(v, turn, 1) if turn else v, high)
            even_pairs[p, t] = jnp.where(upper, low, high)
            odd_pairs[p, t] = jnp.where(upper, high, low)
        for t in range(EDGE, out.shape[1]):
            out[p, t] = jnp.zeros((ny, nz), f32)


def gram_kernel(basis, out, local):
    layers, comps, ny, nz, modes = basis.shape
    slabs = out.shape[0]
    gram = jnp.zeros((modes, modes), f32)
    for x in range(layers):
        for c in range(comps):
            rows = basis[x, c].reshape(ny * nz, modes)
            gram = gram + dot(rows, rows, (0, 0))
    half = modes // 2
    share = half // slabs
    lane = lanes_of((half, modes))
    packed = jnp.where((lane < half) & (lane <= rows_of((half, modes))), pltpu.roll(gram[half:], half, 1), gram[:half])
    own = jnp.sum(jnp.where(rows_of(gram.shape) == lanes_of(gram.shape), gram, 0.0), axis=0, keepdims=True)
    local[...] = jnp.zeros(local.shape, f32)
    local[0:1] = pltpu.roll(own, half, 1)
    local[1:2] = own
    for p in range(slabs):
        for t in range(share // 8):
            out[p, t] = packed[share * p + 8 * t : share * p + 8 * t + 8]


def faces_kernel(odd, block, far, near):
    slabs = block.shape[0]
    first = (rows_of(block.shape[2:]) < REACH).astype(jnp.int32) != odd[0]
    for g in range(slabs):
        for q in range(COUNT + 1):
            a = block[g, 2 * q]
            b = pltpu.roll(block[g, 2 * q + 1], REACH, 0)
            far[g, q] = jnp.where(first, a, b)
            near[g, q] = jnp.where(first, b, a)


def steps_kernel(
    place, odd, drive, moduli, block, far, near, out, share, fields, masks, stiff, weight, couple, diagonal,
    side, side_mask, side_stiff, side_couple, side_diagonal,
):
    slabs, _, ny, nz = block.shape
    nx = 2 * slabs
    first = (rows_of((ny, nz)) < REACH).astype(jnp.int32) == odd[0]
    zero = jnp.zeros((ny, nz), f32)
    plane_zero = jnp.zeros((2 * ny, nz), f32)
    halves = (slice(0, ny), slice(ny, 2 * ny))

    def level_of(value, prop):
        level = zero
        for m in range(moduli.shape[1]):
            level = jnp.where(value == m + 1.0, moduli[prop, m], level)
        return level

    group = lanes_of((ny, nz)) // 16
    sides = {}
    for g in range(slabs):
        edges = [
            (block[g, EDGE], jnp.where(first, far[g, COUNT], near[g, COUNT])),
            (block[g, EDGE + 1], pltpu.roll(jnp.where(first, near[g, COUNT], far[g, COUNT]), REACH, 0)),
        ]
        for q in range(COUNT):
            beside = (
                jnp.where(first, far[g, q], near[g, q]),
                pltpu.roll(jnp.where(first, near[g, q], far[g, q]), REACH, 0),
            )
            for i in range(2):
                x = 2 * g + i
                for rows, value in zip(halves, (block[g, 2 * q + i], beside[i])):
                    if q < FIELDS:
                        fields[0, q, 1 + x, rows] = value
                    elif q < MASKS:
                        fields[1, q - FIELDS, 1 + x, rows] = value
                    elif q < MATERIAL:
                        masks[q - MASKS, x, rows] = value
                    else:
                        stiff[0, 1 + x, rows] = level_of(value, 0)
                        stiff[1, 1 + x, rows] = level_of(value, 1)
                        weight[x, rows] = step_squared * level_of(value, 2)
            if q < MASKS:
                key, cases = (q // FIELDS, q % 3), (q % FIELDS // 3,)
            elif q < MATERIAL:
                key, cases = "mask", (q - MASKS,)
            else:
                key, cases = "material", (0, 1)
            for k in range(2):
                for i in cases:
                    turn = (64 * i + 16 * g - 16 * (q % 8)) % nz
                    edge = edges[q // 8][k]
                    edge = pltpu.roll(edge, turn, 1) if turn else edge
                    sides[key, k] = jnp.where(group == 4 * i + g, edge, sides.get((key, k), zero))
    side_weight = []
    for k, rows in enumerate(halves):
        for t in range(2):
            for c in range(3):
                side[t, c, rows] = sides[(t, c), k]
        side_stiff[0, rows] = level_of(sides["material", k], 0)
        side_stiff[1, rows] = level_of(sides["material", k], 1)
        heavy = step_squared * level_of(sides["material", k], 2)
        side_weight.append(heavy)
        side_mask[rows] = sides["mask", k] * heavy
    for x in (0, nx + 1):
        for f in range(FIELDS):
            fields[0, f, x] = plane_zero
            fields[1, f, x] = plane_zero
        stiff[0, x] = plane_zero
        stiff[1, x] = plane_zero
    for t in range(share.shape[0]):
        total = block[0, GRAM + t]
        for g in range(1, slabs):
            total = total + block[g, GRAM + t]
        share[t] = total

    lane = lanes_of((2 * ny, nz))
    spot = lane % 8
    layer = lane % 64 // 8

    def turned_by(v, shift):
        return pltpu.roll(v, shift % nz, 1) if shift % nz else v

    def near_main(get, edge, base, x, rows):
        v = get(x + 1)
        part = lambda a: a[:rows]
        lanes = lane[:rows]
        low = jnp.where(lanes == 0, turned_by(edge[:rows], -(base + 7)), pltpu.roll(part(v), 1, 1))
        high = jnp.where(lanes == nz - 1, turned_by(edge[:rows], nz - 1 - base), pltpu.roll(part(v), nz - 1, 1))
        return part(v), (
            part(get(x)), part(get(x + 2)), part(pltpu.roll(v, 1, 0)), part(pltpu.roll(v, 2 * ny - 1, 0)), low, high
        )

    def near_side(v, gets):
        low, high = plane_zero, plane_zero
        for i in range(PAIR):
            for x in range(nx):
                base = 64 * i + 8 * x
                main = gets[i](x + 1)
                low = jnp.where(lane == base, turned_by(main, base + 1), low)
                high = jnp.where(lane == base + 7, turned_by(main, base + 7), high)
        return (
            jnp.where(layer == 0, 0.0, pltpu.roll(v, 8, 1)), jnp.where(layer == nx - 1, 0.0, pltpu.roll(v, nz - 8, 1)),
            pltpu.roll(v, 1, 0), pltpu.roll(v, 2 * ny - 1, 0),
            jnp.where(spot == 0, low, pltpu.roll(v, 1, 1)), jnp.where(spot == 7, high, pltpu.roll(v, nz - 1, 1)),
        )

    def coupled(half, kinds, store, store_diagonal):
        sums = []
        for kind in range(2):
            v, near = kinds[kind]
            pairs = []
            for d in range(6):
                value = half * (v + near[d])
                store(kind, d, value)
                pairs.append(value)
            sums.append([pairs[2 * a] + pairs[2 * a + 1] for a in range(3)])
        for c in range(3):
            store_diagonal(c, 2.0 - (sums[0][c] + sums[1][(c + 1) % 3] + sums[1][(c + 2) % 3]))

    def setter(ref, *tail):
        def put(*at):
            ref[at[:-1] + tail] = at[-1]
        return put

    for x in range(nx):
        kinds = [near_main(lambda at: stiff[kind, at], side_stiff[kind], 8 * x, x, 2 * ny) for kind in range(2)]
        coupled(0.5 * weight[x], kinds, setter(couple, x), setter(diagonal, x))
        for i in range(PAIR):
            masks[i, x] = masks[i, x] * weight[x]
    kinds = [(side_stiff[k], near_side(side_stiff[k], [lambda at: stiff[k, at]] * PAIR)) for k in range(2)]
    coupled(0.5 * jnp.concatenate(side_weight), kinds, setter(side_couple), setter(side_diagonal))

    slab = place[0]

    def advanced(v, near, before, centre, forced, pairs, c):
        value = centre * v - before + forced
        for d in range(6):
            value = value + pairs(0 if d // 2 == c else 1, d) * near[d]
        return value

    for s in range(STEPS):
        ramp = min(1.0, (s + 1) / ramp_steps)
        last = s == STEPS - 1
        rows = ny if last else 2 * ny
        now, to = s % 2, 1 - s % 2
        force = [[drive[c, PAIR * slab + i] * ramp for c in range(3)] for i in range(PAIR)]
        for c in range(3):
            gets = [lambda at, f=3 * i + c: fields[now, f, at] for i in range(PAIR)]
            edge = side[now, c]
            if not last:
                push = jnp.where(lane < 64, force[0][c], force[1][c])
                side[to, c] = advanced(
                    edge, near_side(edge, gets), side[to, c], side_diagonal[c], side_mask[...] * push,
                    lambda kind, d: side_couple[kind, d], c,
                )
            for x in range(nx):
                for i in range(PAIR):
                    f = 3 * i + c
                    v, near = near_main(gets[i], edge, 64 * i + 8 * x, x, rows)
                    value = advanced(
                        v, near, fields[to, f, x + 1, :rows], diagonal[c, x, :rows], masks[i, x, :rows] * force[i][c],
                        lambda kind, d: couple[kind, d, x, :rows], c,
                    )
                    if not last:
                        fields[to, f, x + 1] = value
                    out[x // 2, s, f, x % 2] = value[:ny]


def project_kernel(basis, states, share, local, out, stage):
    layers, comps, ny, nz, modes = basis.shape
    count = STEPS * CASES
    coef = jnp.zeros((count, modes), f32)
    square = jnp.zeros((count, count), f32)
    for x in range(layers):
        for c in range(comps):
            at = x * comps + c
            for s in range(STEPS):
                for j in range(CASES):
                    r = s * CASES + j
                    stage[at, r * ny : (r + 1) * ny, :] = states[j // PAIR, s, (j % PAIR) * comps + c, x]
            block = jnp.concatenate(
                [stage[at, pl.ds(y, count, stride=ny), :].astype(bf16) for y in range(ny)], axis=1
            )
            coef = coef + dot(block, basis[x, c].reshape(ny * nz, modes), (1, 0))
            square = square + dot(block, block, (1, 1))
    lane = lanes_of((CASES, count))
    tile = jnp.zeros((CASES, count), f32)
    for s in range(STEPS):
        tile = jnp.where(lane // CASES == s, square[s * CASES : (s + 1) * CASES], tile)
    tile = jnp.concatenate([tile, jnp.zeros((CASES, modes - count), f32)], axis=1)
    tile = jnp.where(lanes_of(tile.shape) < modes // 2, tile, local[...])
    half = count // 2
    for g in range(out.shape[0]):
        h = g % 2
        out[g, :half] = coef[h * half : (h + 1) * half]
        out[g, half : half + CASES] = tile
        out[g, half + CASES :] = share[h]


def sum_kernel(parts, out):
    total = parts[0]
    for g in range(1, parts.shape[0]):
        total = total + parts[g]
    for g in range(out.shape[0]):
        out[g] = total


def factor(gram):
    rows = rows_of(gram.shape)
    lane = lanes_of(gram.shape)
    work = jnp.where(lane < CASES, gram, jnp.where(lane == rows + CASES, 1.0, 0.0))
    for p in range(CASES - 1):
        ratio = work[:, p : p + 1] * (1.0 / work[p : p + 1, p : p + 1])
        work = work - jnp.where(rows > p, ratio, 0.0) * work[p : p + 1]
    pivots = jnp.sum(jnp.where(lane == rows, work, 0.0), axis=1, keepdims=True)
    work = work * (1.0 / jnp.sqrt(pivots))
    upper = jnp.where((rows <= lane) & (lane < CASES), work, 0.0)
    inverse = jnp.where(lane < CASES, pltpu.roll(work, gram.shape[1] - CASES, 1), 0.0)
    return upper, inverse


def mixed(small, rows):
    total = small[:, :1] * rows[:1]
    for i in range(1, CASES):
        total = total + small[:, i : i + 1] * rows[i : i + 1]
    return total


def padded(rows):
    return jnp.concatenate([rows, jnp.zeros((rows.shape[1] - rows.shape[0], rows.shape[1]), f32)])


def pieces_of(value):
    pieces = []
    for _ in range(3):
        piece = value.astype(bf16)
        pieces.append(piece)
        value = value - piece.astype(f32)
    return pieces


def exact(rounded, pieces, contract):
    total = dot(rounded, pieces[2], contract)
    return total + dot(rounded, pieces[1], contract) + dot(rounded, pieces[0], contract)


def finish_kernel(weight, parts, basis, states, displacement, modes_out, coefficients, factors, stage, held, sems):
    layers, comps, ny, nz, modes = basis.shape
    moved = []
    for c in range(comps):
        for j in range(CASES):
            moved.append(pltpu.make_async_copy(
                states.at[j // PAIR, STEPS - 1, (j % PAIR) * comps + c], displacement.at[c, j], sems.at[len(moved)]
            ))
            moved[-1].start()
    count = STEPS * CASES
    half = modes // 2
    high = lax.Precision.HIGHEST
    members, upto = parts.shape[0], count // 2 + CASES
    owns = []
    for h in range(2):
        own = parts[h, :upto]
        for g in range(h + 2, members, 2):
            own = own + parts[g, :upto]
        owns.append(own * weight)
    coef = jnp.concatenate([own[: count // 2] for own in owns])
    square = owns[0][count // 2 :]
    packed = jnp.concatenate([parts[g, upto:] for g in range(members)]) * weight
    lane, row = lanes_of(packed.shape), rows_of(packed.shape)
    flipped = padded(packed).T
    diagonal = jnp.where(lane[:1] < half, pltpu.roll(square[:1], half, 1), square[1:2])
    top = jnp.where(lane < row, flipped[:half], packed)
    top = jnp.where(lane == row, diagonal, top)
    bottom = jnp.where(lane - half <= row, pltpu.roll(packed, half, 1), pltpu.roll(flipped[:half], half, 1))
    bottom = jnp.where(lane < half, flipped[half:], bottom)
    bottom = jnp.where(lane - half == row, diagonal, bottom)
    gram = pieces_of(jnp.concatenate([top, bottom]))
    lane = lanes_of(square.shape)

    def block_of(rows, s):
        turn = (modes - s * CASES) % modes
        rows = pltpu.roll(rows, turn, 1) if turn else rows
        return jnp.where(lane < CASES, rows, 0.0)

    def change_of(coef):
        rounded = coef.astype(bf16)
        left = coef - exact(rounded, gram, (1, 0))
        wide = padded(rounded.astype(f32)).astype(bf16)
        change = exact(rounded, pieces_of(padded(left)), (1, 1))
        for piece in pieces_of(coef)[::-1]:
            change = change + dot(piece, wide, (1, 1))
        return rounded.astype(f32), left, change

    def expanded(rounded, slot):
        for c in range(comps):
            for x in range(layers):
                at = x * comps + c
                taken = dot(rounded.astype(bf16), basis[x, c].reshape(ny * nz, modes), (1, 1))
                for y in range(ny):
                    stage[slot, at, pl.ds(y, CASES, stride=ny), :] = taken[:, y * nz : (y + 1) * nz]

    rounded, left, change = change_of(coef)
    expanded(rounded[count - CASES :], 0)
    first, second = [], []
    for s in range(STEPS):
        at = slice(s * CASES, (s + 1) * CASES)
        first.append(factor(block_of(square - change[at], s)))
        second.append(mixed(first[s][1], left[at]))
    second = jnp.concatenate(second)
    rounded_2, left_2, change = change_of(second)
    expanded(rounded_2[count - CASES :], 1)
    for s in range(STEPS):
        at = slice(s * CASES, (s + 1) * CASES)
        whole = dot(first[s][0], padded(first[s][1]), (1, 1), high)
        upper, inverse = factor(whole - block_of(change[at], s))
        factors[s] = mixed(upper, first[s][0])[:, :CASES]
        coefficients[s, 0] = coef[at]
        coefficients[s, 1] = second[at]
    mix = mixed(inverse, first[-1][1])
    wide = lambda small: [
        [jnp.broadcast_to(small[i : i + 1, j : j + 1], (ny, nz)) for j in range(i + 1)] for i in range(CASES)
    ]
    mix, inverse = wide(mix), wide(inverse)
    for c in range(comps):
        for x in range(layers):
            at = x * comps + c
            resid, extra = [], []
            for j in range(CASES):
                here = slice(j * ny, (j + 1) * ny)
                snapshot = states[j // PAIR, STEPS - 1, (j % PAIR) * comps + c, x].astype(bf16).astype(f32)
                resid.append(snapshot - stage[0, at, here])
                extra.append(stage[1, at, here])
            for i in range(CASES):
                total = mix[i][0] * resid[0] - inverse[i][0] * extra[0]
                for j in range(1, i + 1):
                    total = total + (mix[i][j] * resid[j] - inverse[i][j] * extra[j])
                held[c, i, x] = total
        moved.append(pltpu.make_async_copy(held.at[c], modes_out.at[c], sems.at[len(moved)]))
        moved[-1].start()
    for copy in moved:
        copy.wait()


def call(kernel, outs, inputs, scratch=(), scalars=0, copies=0, ins_away=0, outs_away=0, room=40):
    vmem = pl.BlockSpec(memory_space=pltpu.VMEM)
    smem = pl.BlockSpec(memory_space=pltpu.SMEM)
    away = pl.BlockSpec(memory_space=pltpu.HBM)
    scratch = [pltpu.VMEM(shape, f32) if isinstance(shape, tuple) else shape for shape in scratch]
    return pl.pallas_call(
        kernel,
        out_shape=[jax.ShapeDtypeStruct(shape, f32) if isinstance(shape, tuple) else shape for shape in outs],
        in_specs=[smem] * scalars + [away] * ins_away + [vmem] * (len(inputs) - scalars - ins_away),
        out_specs=[away] * outs_away + [vmem] * (len(outs) - outs_away),
        scratch_shapes=scratch + ([pltpu.SemaphoreType.DMA((copies,))] if copies else []),
        compiler_params=pltpu.CompilerParams(vmem_limit_bytes=room << 20),
    )(*inputs)


def swapped(block, axis, start):
    pairs = [(i, i + 1) for i in range(start, lax.axis_size(axis) - 1, 2)]
    return lax.ppermute(block, axis, pairs + [(b, a) for a, b in pairs])


def turned(parts, axis):
    return lax.all_to_all(parts, axis, 0, 0, tiled=True)


def shards(basis, modal_now, modal_prev, material_ids, moduli, drive_mask, drive):
    layers, comps, ny, nz, modes = basis.shape
    slabs, rows, depth = (lax.axis_size(a) for a in ("gx", "gy", "gz"))
    dof_weight = 1.0 / (3.0 * layers * ny * nz * slabs * rows * depth)
    tile = (ny, nz)
    share = modes // 2 // slabs // 8
    blocks = layers * comps
    inputs = [pltpu.with_memory_space_constraint(a, pltpu.HBM) for a in (modal_now.T, modal_prev.T, basis, material_ids, drive_mask)]
    place = lax.axis_index("gx").astype(jnp.int32)[None]
    odd = (lax.axis_index("gy") & 1).astype(jnp.int32)[None]
    above_z = (lax.axis_index("gz") & 1).astype(jnp.int32)[None]
    block, even_pairs, odd_pairs, basis = call(
        start_kernel,
        [(slabs, GRAM + share) + tile, (slabs, 2) + tile, (slabs, 2) + tile, jax.ShapeDtypeStruct(basis.shape, bf16)],
        [place, odd, above_z] + inputs,
        [pltpu.VMEM(a.shape, a.dtype) for i, a in enumerate(inputs) if i != 2] + [(blocks, 2 * CASES * ny, nz)],
        scalars=3,
        copies=blocks + 4,
        ins_away=5,
    )
    edge = swapped(even_pairs, "gz", 0) + swapped(odd_pairs, "gz", 1)
    gram, local = call(gram_kernel, [(slabs, share) + tile, (CASES, modes)], [basis])
    block = lax.dynamic_update_slice(block, jnp.concatenate([edge, gram], axis=1), (0, EDGE, 0, 0))
    block = turned(block, "gx")
    far, near = call(faces_kernel, [(slabs, COUNT + 1) + tile] * 2, [odd, block], scalars=1)
    far = swapped(far, "gy", 1)
    near = swapped(near, "gy", 0)
    nx = layers * slabs
    wide = (2 * ny, nz)
    states, gram = call(
        steps_kernel,
        [(slabs, STEPS, FIELDS, layers) + tile, (share,) + tile],
        [place, odd, drive, moduli, block, far, near],
        [
            (2, FIELDS, nx + 2) + wide, (PAIR, nx) + wide, (2, nx + 2) + wide, (nx,) + wide,
            (2, 6, nx) + wide, (3, nx) + wide, (2, 3) + wide, wide, (2,) + wide, (2, 6) + wide, (3,) + wide,
        ],
        4,
    )
    states = turned(states, "gx")
    count = STEPS * CASES
    width = count // 2 + CASES + 8
    parts, = call(
        project_kernel, [(rows, width, modes)], [basis, states, gram, local], [(blocks, count * ny, nz)]
    )
    parts, = call(sum_kernel, [(depth, width, modes)], [turned(parts, "gy")])
    parts, = call(sum_kernel, [(2 * slabs, width, modes)], [turned(parts, "gz")])
    groups = [
        [(a * rows + 2 * h + core) * depth + z for a in range(slabs) for core in range(2)]
        for h in range(rows // 2)
        for z in range(depth)
    ]
    parts = lax.all_to_all(parts, ("gx", "gy", "gz"), 0, 0, tiled=True, axis_index_groups=groups)
    held = (comps, CASES, layers) + tile
    displacement, modes_out, coefficients, factors = call(
        lambda *refs: finish_kernel(dof_weight, *refs),
        [held, held, (STEPS, 2, CASES, modes), (STEPS, CASES, CASES)],
        [parts, basis, states],
        [(2, blocks, CASES * ny, nz), held],
        copies=comps * CASES + comps,
        outs_away=2,
    )
    return displacement, modes_out, coefficients.transpose(0, 1, 3, 2), factors


def solution(mesh):
    in_specs = (
        P("gx", None, "gy", "gz", None),
        P(),
        P(),
        P("gx", "gy", "gz"),
        P(),
        P(None, "gx", "gy", "gz"),
        P(),
    )
    out_specs = (P(None, None, "gx", "gy", "gz"), P(None, None, "gx", "gy", "gz"), P(), P())
    return jax.shard_map(
        shards, mesh=mesh, in_specs=in_specs, out_specs=out_specs, check_vma=False
    )
```

```python
import jax
import jax.numpy as jnp
from jax import lax
from jax.experimental import pallas as pl
from jax.experimental.pallas import tpu as pltpu
from jax.sharding import PartitionSpec as P

STEPS = 4
SHARES = 4
CASES = 8
step_squared = 0.1
ramp_steps = 4.0

PAIR = 2
FIELDS = 3 * PAIR
MASKS = 2 * FIELDS
MATERIAL = MASKS + PAIR
COUNT = MATERIAL + 1
EDGE = 2 * COUNT
GRAM = EDGE + 2
REACH = 4
f32 = jnp.float32
bf16 = jnp.bfloat16


def dot(a, b, contract, precision=None):
    return lax.dot_general(
        a, b, ((contract[:1], contract[1:]), ((), ())),
        precision=precision, preferred_element_type=f32,
    )


def lanes_of(shape):
    return lax.broadcasted_iota(jnp.int32, shape, len(shape) - 1)


def rows_of(shape):
    return lax.broadcasted_iota(jnp.int32, shape, len(shape) - 2)


def start_kernel(place, odd, turn_z, now, prev, basis, ids, mask, out, even_pairs, odd_pairs, basis_in, now_in, prev_in, ids_in, mask_in, stage, sems):
    layers, comps, ny, nz, modes = basis.shape
    slabs = out.shape[0]
    moved = [(now, now_in), (prev, prev_in)]
    moved += [(basis.at[x, c], basis_in.at[x, c]) for x in range(layers) for c in range(comps)]
    moved += [(ids, ids_in), (mask, mask_in)]
    moved = [pltpu.make_async_copy(*pair, sems.at[k]) for k, pair in enumerate(moved)]
    for copy in moved:
        copy.start()
    moved[0].wait()
    moved[1].wait()
    modal = jnp.concatenate([now_in[...].astype(f32), prev_in[...].astype(f32)]).astype(bf16)
    for x in range(layers):
        for c in range(comps):
            at = x * comps + c
            moved[2 + at].wait()
            rows = basis_in[x, c].reshape(ny * nz, modes)
            both = dot(modal, rows, (1, 1))
            for y in range(ny):
                stage[at, pl.ds(y, 2 * CASES, stride=ny), :] = both[:, y * nz : (y + 1) * nz]
            for r in range(2 * CASES):
                j = r % CASES
                field = (r // CASES) * FIELDS + (j % PAIR) * comps + c
                out[j // PAIR, 2 * field + x] = stage[at, r * ny : (r + 1) * ny, :]
    moved[-2].wait()
    moved[-1].wait()
    for p in range(slabs):
        for x in range(layers):
            for i in range(PAIR):
                out[p, 2 * (MASKS + i) + x] = mask_in[PAIR * p + i, x].astype(f32)
            out[p, 2 * MATERIAL + x] = (ids_in[x] + 1).astype(f32)
        quarter = lanes_of((ny, nz)) // REACH
        upper = jnp.full((ny, nz), turn_z[0], jnp.int32) == 1
        for t in range(2):
            low = jnp.zeros((ny, nz), f32)
            high = jnp.zeros((ny, nz), f32)
            for g in range(16):
                tile = 16 * t + g
                if tile < 2 * COUNT:
                    v = out[p, tile]
                    low = jnp.where(quarter == 2 * g, pltpu.roll(v, 8 * g, 1) if g else v, low)
                    turn = (8 * g + 8) % nz
                    high = jnp.where(quarter == 2 * g + 1, pltpu.roll(v, turn, 1) if turn else v, high)
            even_pairs[p, t] = jnp.where(upper, low, high)
            odd_pairs[p, t] = jnp.where(upper, high, low)
        for t in range(EDGE, out.shape[1]):
            out[p, t] = jnp.zeros((ny, nz), f32)


def gram_kernel(basis, out, local):
    layers, comps, ny, nz, modes = basis.shape
    slabs = out.shape[0]
    gram = jnp.zeros((modes, modes), f32)
    for x in range(layers):
        for c in range(comps):
            rows = basis[x, c].reshape(ny * nz, modes)
            gram = gram + dot(rows, rows, (0, 0))
    half = modes // 2
    share = half // slabs
    lane = lanes_of((half, modes))
    packed = jnp.where((lane < half) & (lane <= rows_of((half, modes))), pltpu.roll(gram[half:], half, 1), gram[:half])
    own = jnp.sum(jnp.where(rows_of(gram.shape) == lanes_of(gram.shape), gram, 0.0), axis=0, keepdims=True)
    local[...] = jnp.zeros(local.shape, f32)
    local[0:1] = pltpu.roll(own, half, 1)
    local[1:2] = own
    for p in range(slabs):
        for t in range(share // 8):
            out[p, t] = packed[share * p + 8 * t : share * p + 8 * t + 8]


def faces_kernel(odd, block, far, near):
    slabs = block.shape[0]
    first = (rows_of(block.shape[2:]) < REACH).astype(jnp.int32) != odd[0]
    for g in range(slabs):
        for q in range(COUNT + 1):
            a = block[g, 2 * q]
            b = pltpu.roll(block[g, 2 * q + 1], REACH, 0)
            far[g, q] = jnp.where(first, a, b)
            near[g, q] = jnp.where(first, b, a)


def steps_kernel(
    place, odd, drive, moduli, block, far, near, out, share, fields, masks, stiff, weight, couple, diagonal,
    side, side_mask, side_stiff, side_couple, side_diagonal,
):
    slabs, _, ny, nz = block.shape
    nx = 2 * slabs
    first = (rows_of((ny, nz)) < REACH).astype(jnp.int32) == odd[0]
    zero = jnp.zeros((ny, nz), f32)
    plane_zero = jnp.zeros((2 * ny, nz), f32)
    halves = (slice(0, ny), slice(ny, 2 * ny))

    def level_of(value, prop):
        level = zero
        for m in range(moduli.shape[1]):
            level = jnp.where(value == m + 1.0, moduli[prop, m], level)
        return level

    group = lanes_of((ny, nz)) // 16
    sides = {}
    for g in range(slabs):
        edges = [
            (block[g, EDGE], jnp.where(first, far[g, COUNT], near[g, COUNT])),
            (block[g, EDGE + 1], pltpu.roll(jnp.where(first, near[g, COUNT], far[g, COUNT]), REACH, 0)),
        ]
        for q in range(COUNT):
            beside = (
                jnp.where(first, far[g, q], near[g, q]),
                pltpu.roll(jnp.where(first, near[g, q], far[g, q]), REACH, 0),
            )
            for i in range(2):
                x = 2 * g + i
                for rows, value in zip(halves, (block[g, 2 * q + i], beside[i])):
                    if q < FIELDS:
                        fields[0, q, 1 + x, rows] = value
                    elif q < MASKS:
                        fields[1, q - FIELDS, 1 + x, rows] = value
                    elif q < MATERIAL:
                        masks[q - MASKS, x, rows] = value
                    else:
                        stiff[0, 1 + x, rows] = level_of(value, 0)
                        stiff[1, 1 + x, rows] = level_of(value, 1)
                        weight[x, rows] = step_squared * level_of(value, 2)
            if q < MASKS:
                key, cases = (q // FIELDS, q % 3), (q % FIELDS // 3,)
            elif q < MATERIAL:
                key, cases = "mask", (q - MASKS,)
            else:
                key, cases = "material", (0, 1)
            for k in range(2):
                for i in cases:
                    turn = (64 * i + 16 * g - 16 * (q % 8)) % nz
                    edge = edges[q // 8][k]
                    edge = pltpu.roll(edge, turn, 1) if turn else edge
                    sides[key, k] = jnp.where(group == 4 * i + g, edge, sides.get((key, k), zero))
    side_weight = []
    for k, rows in enumerate(halves):
        for t in range(2):
            for c in range(3):
                side[t, c, rows] = sides[(t, c), k]
        side_stiff[0, rows] = level_of(sides["material", k], 0)
        side_stiff[1, rows] = level_of(sides["material", k], 1)
        heavy = step_squared * level_of(sides["material", k], 2)
        side_weight.append(heavy)
        side_mask[rows] = sides["mask", k] * heavy
    for x in (0, nx + 1):
        for f in range(FIELDS):
            fields[0, f, x] = plane_zero
            fields[1, f, x] = plane_zero
        stiff[0, x] = plane_zero
        stiff[1, x] = plane_zero
    for t in range(share.shape[0]):
        total = block[0, GRAM + t]
        for g in range(1, slabs):
            total = total + block[g, GRAM + t]
        share[t] = total

    lane = lanes_of((2 * ny, nz))
    spot = lane % 8
    layer = lane % 64 // 8

    def turned_by(v, shift):
        return pltpu.roll(v, shift % nz, 1) if shift % nz else v

    def near_main(get, edge, base, x, rows):
        v = get(x + 1)
        part = lambda a: a[:rows]
        lanes = lane[:rows]
        low = jnp.where(lanes == 0, turned_by(edge[:rows], -(base + 7)), pltpu.roll(part(v), 1, 1))
        high = jnp.where(lanes == nz - 1, turned_by(edge[:rows], nz - 1 - base), pltpu.roll(part(v), nz - 1, 1))
        return part(v), (
            part(get(x)), part(get(x + 2)), part(pltpu.roll(v, 1, 0)), part(pltpu.roll(v, 2 * ny - 1, 0)), low, high
        )

    def near_side(v, gets):
        low, high = plane_zero, plane_zero
        for i in range(PAIR):
            for x in range(nx):
                base = 64 * i + 8 * x
                main = gets[i](x + 1)
                low = jnp.where(lane == base, turned_by(main, base + 1), low)
                high = jnp.where(lane == base + 7, turned_by(main, base + 7), high)
        return (
            jnp.where(layer == 0, 0.0, pltpu.roll(v, 8, 1)), jnp.where(layer == nx - 1, 0.0, pltpu.roll(v, nz - 8, 1)),
            pltpu.roll(v, 1, 0), pltpu.roll(v, 2 * ny - 1, 0),
            jnp.where(spot == 0, low, pltpu.roll(v, 1, 1)), jnp.where(spot == 7, high, pltpu.roll(v, nz - 1, 1)),
        )

    def coupled(half, kinds, store, store_diagonal):
        sums = []
        for kind in range(2):
            v, near = kinds[kind]
            pairs = []
            for d in range(6):
                value = half * (v + near[d])
                store(kind, d, value)
                pairs.append(value)
            sums.append([pairs[2 * a] + pairs[2 * a + 1] for a in range(3)])
        for c in range(3):
            store_diagonal(c, 2.0 - (sums[0][c] + sums[1][(c + 1) % 3] + sums[1][(c + 2) % 3]))

    def setter(ref, *tail):
        def put(*at):
            ref[at[:-1] + tail] = at[-1]
        return put

    for x in range(nx):
        kinds = [near_main(lambda at: stiff[kind, at], side_stiff[kind], 8 * x, x, 2 * ny) for kind in range(2)]
        coupled(0.5 * weight[x], kinds, setter(couple, x), setter(diagonal, x))
        for i in range(PAIR):
            masks[i, x] = masks[i, x] * weight[x]
    kinds = [(side_stiff[k], near_side(side_stiff[k], [lambda at: stiff[k, at]] * PAIR)) for k in range(2)]
    coupled(0.5 * jnp.concatenate(side_weight), kinds, setter(side_couple), setter(side_diagonal))

    slab = place[0]

    def advanced(v, near, before, centre, forced, pairs, c):
        value = centre * v - before + forced
        for d in range(6):
            value = value + pairs(0 if d // 2 == c else 1, d) * near[d]
        return value

    for s in range(STEPS):
        ramp = min(1.0, (s + 1) / ramp_steps)
        last = s == STEPS - 1
        rows = ny if last else 2 * ny
        now, to = s % 2, 1 - s % 2
        force = [[drive[c, PAIR * slab + i] * ramp for c in range(3)] for i in range(PAIR)]
        for c in range(3):
            gets = [lambda at, f=3 * i + c: fields[now, f, at] for i in range(PAIR)]
            edge = side[now, c]
            if not last:
                push = jnp.where(lane < 64, force[0][c], force[1][c])
                side[to, c] = advanced(
                    edge, near_side(edge, gets), side[to, c], side_diagonal[c], side_mask[...] * push,
                    lambda kind, d: side_couple[kind, d], c,
                )
            for x in range(nx):
                for i in range(PAIR):
                    f = 3 * i + c
                    v, near = near_main(gets[i], edge, 64 * i + 8 * x, x, rows)
                    value = advanced(
                        v, near, fields[to, f, x + 1, :rows], diagonal[c, x, :rows], masks[i, x, :rows] * force[i][c],
                        lambda kind, d: couple[kind, d, x, :rows], c,
                    )
                    if not last:
                        fields[to, f, x + 1] = value
                    out[x // 2, s, f, x % 2] = value[:ny]


def project_kernel(basis, states, share, local, out, stage):
    layers, comps, ny, nz, modes = basis.shape
    count = STEPS * CASES
    coef = jnp.zeros((count, modes), f32)
    square = jnp.zeros((count, count), f32)
    for x in range(layers):
        for c in range(comps):
            at = x * comps + c
            for s in range(STEPS):
                for j in range(CASES):
                    r = s * CASES + j
                    stage[at, r * ny : (r + 1) * ny, :] = states[j // PAIR, s, (j % PAIR) * comps + c, x]
            block = jnp.concatenate(
                [stage[at, pl.ds(y, count, stride=ny), :].astype(bf16) for y in range(ny)], axis=1
            )
            coef = coef + dot(block, basis[x, c].reshape(ny * nz, modes), (1, 0))
            square = square + dot(block, block, (1, 1))
    lane = lanes_of((CASES, count))
    tile = jnp.zeros((CASES, count), f32)
    for s in range(STEPS):
        tile = jnp.where(lane // CASES == s, square[s * CASES : (s + 1) * CASES], tile)
    tile = jnp.concatenate([tile, jnp.zeros((CASES, modes - count), f32)], axis=1)
    tile = jnp.where(lanes_of(tile.shape) < modes // 2, tile, local[...])
    both = jnp.concatenate([share[t] for t in range(share.shape[0])])
    for g in range(out.shape[0]):
        k = g * SHARES // out.shape[0]
        pieces = [v[k * len(v) // SHARES : (k + 1) * len(v) // SHARES] for v in (coef, tile, both)]
        used = sum(len(v) for v in pieces)
        pieces.append(jnp.zeros((out.shape[1] - used, modes), f32))
        out[g] = jnp.concatenate(pieces)


def sum_kernel(parts, out):
    total = parts[0]
    for g in range(1, parts.shape[0]):
        total = total + parts[g]
    for g in range(out.shape[0]):
        out[g] = total


def factor(gram):
    rows = rows_of(gram.shape)
    lane = lanes_of(gram.shape)
    work = jnp.where(lane < CASES, gram, jnp.where(lane == rows + CASES, 1.0, 0.0))
    for p in range(CASES - 1):
        ratio = work[:, p : p + 1] * (1.0 / work[p : p + 1, p : p + 1])
        work = work - jnp.where(rows > p, ratio, 0.0) * work[p : p + 1]
    pivots = jnp.sum(jnp.where(lane == rows, work, 0.0), axis=1, keepdims=True)
    work = work * (1.0 / jnp.sqrt(pivots))
    upper = jnp.where((rows <= lane) & (lane < CASES), work, 0.0)
    inverse = jnp.where(lane < CASES, pltpu.roll(work, gram.shape[1] - CASES, 1), 0.0)
    return upper, inverse


def mixed(small, rows):
    total = small[:, :1] * rows[:1]
    for i in range(1, CASES):
        total = total + small[:, i : i + 1] * rows[i : i + 1]
    return total


def padded(rows):
    return jnp.concatenate([rows, jnp.zeros((rows.shape[1] - rows.shape[0], rows.shape[1]), f32)])


def pieces_of(value):
    pieces = []
    for _ in range(3):
        piece = value.astype(bf16)
        pieces.append(piece)
        value = value - piece.astype(f32)
    return pieces


def exact(rounded, pieces, contract):
    total = dot(rounded, pieces[2], contract)
    return total + dot(rounded, pieces[1], contract) + dot(rounded, pieces[0], contract)


def finish_kernel(weight, parts, basis, states, displacement, modes_out, coefficients, factors, stage, held, sems):
    layers, comps, ny, nz, modes = basis.shape
    moved = []
    for c in range(comps):
        for j in range(CASES):
            moved.append(pltpu.make_async_copy(
                states.at[j // PAIR, STEPS - 1, (j % PAIR) * comps + c], displacement.at[c, j], sems.at[len(moved)]
            ))
            moved[-1].start()
    count = STEPS * CASES
    half = modes // 2
    high = lax.Precision.HIGHEST
    members = parts.shape[0] // SHARES
    ends = (count // SHARES, (count + CASES) // SHARES, (count + CASES + 2 * CASES) // SHARES)
    owns = []
    for k in range(SHARES):
        own = parts[k]
        for g in range(1, members):
            own = own + parts[g * SHARES + k]
        owns.append(own * weight)
    coef = jnp.concatenate([own[: ends[0]] for own in owns])
    square = jnp.concatenate([own[ends[0] : ends[1]] for own in owns])
    packed = [parts[g * SHARES + k, ends[1] : ends[2]] for g in range(members) for k in range(SHARES)]
    packed = jnp.concatenate(packed) * weight
    lane, row = lanes_of(packed.shape), rows_of(packed.shape)
    flipped = padded(packed).T
    diagonal = jnp.where(lane[:1] < half, pltpu.roll(square[:1], half, 1), square[1:2])
    top = jnp.where(lane < row, flipped[:half], packed)
    top = jnp.where(lane == row, diagonal, top)
    bottom = jnp.where(lane - half <= row, pltpu.roll(packed, half, 1), pltpu.roll(flipped[:half], half, 1))
    bottom = jnp.where(lane < half, flipped[half:], bottom)
    bottom = jnp.where(lane - half == row, diagonal, bottom)
    gram = pieces_of(jnp.concatenate([top, bottom]))
    lane = lanes_of(square.shape)

    def block_of(rows, s):
        turn = (modes - s * CASES) % modes
        rows = pltpu.roll(rows, turn, 1) if turn else rows
        return jnp.where(lane < CASES, rows, 0.0)

    def change_of(coef):
        rounded = coef.astype(bf16)
        left = coef - exact(rounded, gram, (1, 0))
        wide = padded(rounded.astype(f32)).astype(bf16)
        change = exact(rounded, pieces_of(padded(left)), (1, 1))
        for piece in pieces_of(coef)[::-1]:
            change = change + dot(piece, wide, (1, 1))
        return rounded.astype(f32), left, change

    def expanded(rounded, slot):
        for c in range(comps):
            for x in range(layers):
                at = x * comps + c
                taken = dot(rounded.astype(bf16), basis[x, c].reshape(ny * nz, modes), (1, 1))
                for y in range(ny):
                    stage[slot, at, pl.ds(y, CASES, stride=ny), :] = taken[:, y * nz : (y + 1) * nz]

    rounded, left, change = change_of(coef)
    expanded(rounded[count - CASES :], 0)
    first, second = [], []
    for s in range(STEPS):
        at = slice(s * CASES, (s + 1) * CASES)
        first.append(factor(block_of(square - change[at], s)))
        second.append(mixed(first[s][1], left[at]))
    second = jnp.concatenate(second)
    rounded_2, left_2, change = change_of(second)
    expanded(rounded_2[count - CASES :], 1)
    for s in range(STEPS):
        at = slice(s * CASES, (s + 1) * CASES)
        whole = dot(first[s][0], padded(first[s][1]), (1, 1), high)
        upper, inverse = factor(whole - block_of(change[at], s))
        factors[s] = mixed(upper, first[s][0])[:, :CASES]
        coefficients[s, 0] = coef[at]
        coefficients[s, 1] = second[at]
    mix = mixed(inverse, first[-1][1])
    wide = lambda small: [
        [jnp.broadcast_to(small[i : i + 1, j : j + 1], (ny, nz)) for j in range(i + 1)] for i in range(CASES)
    ]
    mix, inverse = wide(mix), wide(inverse)
    for c in range(comps):
        for x in range(layers):
            at = x * comps + c
            resid, extra = [], []
            for j in range(CASES):
                here = slice(j * ny, (j + 1) * ny)
                snapshot = states[j // PAIR, STEPS - 1, (j % PAIR) * comps + c, x].astype(bf16).astype(f32)
                resid.append(snapshot - stage[0, at, here])
                extra.append(stage[1, at, here])
            for i in range(CASES):
                total = mix[i][0] * resid[0] - inverse[i][0] * extra[0]
                for j in range(1, i + 1):
                    total = total + (mix[i][j] * resid[j] - inverse[i][j] * extra[j])
                held[c, i, x] = total
        moved.append(pltpu.make_async_copy(held.at[c], modes_out.at[c], sems.at[len(moved)]))
        moved[-1].start()
    for copy in moved:
        copy.wait()


def call(kernel, outs, inputs, scratch=(), scalars=0, copies=0, ins_away=0, outs_away=0, room=40):
    vmem = pl.BlockSpec(memory_space=pltpu.VMEM)
    smem = pl.BlockSpec(memory_space=pltpu.SMEM)
    away = pl.BlockSpec(memory_space=pltpu.HBM)
    scratch = [pltpu.VMEM(shape, f32) if isinstance(shape, tuple) else shape for shape in scratch]
    return pl.pallas_call(
        kernel,
        out_shape=[jax.ShapeDtypeStruct(shape, f32) if isinstance(shape, tuple) else shape for shape in outs],
        in_specs=[smem] * scalars + [away] * ins_away + [vmem] * (len(inputs) - scalars - ins_away),
        out_specs=[away] * outs_away + [vmem] * (len(outs) - outs_away),
        scratch_shapes=scratch + ([pltpu.SemaphoreType.DMA((copies,))] if copies else []),
        compiler_params=pltpu.CompilerParams(vmem_limit_bytes=room << 20),
    )(*inputs)


def swapped(block, axis, start):
    pairs = [(i, i + 1) for i in range(start, lax.axis_size(axis) - 1, 2)]
    return lax.ppermute(block, axis, pairs + [(b, a) for a, b in pairs])


def turned(parts, axis):
    return lax.all_to_all(parts, axis, 0, 0, tiled=True)


def shards(basis, modal_now, modal_prev, material_ids, moduli, drive_mask, drive):
    layers, comps, ny, nz, modes = basis.shape
    slabs, rows, depth = (lax.axis_size(a) for a in ("gx", "gy", "gz"))
    dof_weight = 1.0 / (3.0 * layers * ny * nz * slabs * rows * depth)
    tile = (ny, nz)
    share = modes // 2 // slabs // 8
    blocks = layers * comps
    inputs = [pltpu.with_memory_space_constraint(a, pltpu.HBM) for a in (modal_now.T, modal_prev.T, basis, material_ids, drive_mask)]
    place = lax.axis_index("gx").astype(jnp.int32)[None]
    odd = (lax.axis_index("gy") & 1).astype(jnp.int32)[None]
    above_z = (lax.axis_index("gz") & 1).astype(jnp.int32)[None]
    block, even_pairs, odd_pairs, basis = call(
        start_kernel,
        [(slabs, GRAM + share) + tile, (slabs, 2) + tile, (slabs, 2) + tile, jax.ShapeDtypeStruct(basis.shape, bf16)],
        [place, odd, above_z] + inputs,
        [pltpu.VMEM(a.shape, a.dtype) for i, a in enumerate(inputs) if i != 2] + [(blocks, 2 * CASES * ny, nz)],
        scalars=3,
        copies=blocks + 4,
        ins_away=5,
    )
    edge = swapped(even_pairs, "gz", 0) + swapped(odd_pairs, "gz", 1)
    gram, local = call(gram_kernel, [(slabs, share) + tile, (CASES, modes)], [basis])
    block = lax.dynamic_update_slice(block, jnp.concatenate([edge, gram], axis=1), (0, EDGE, 0, 0))
    block = turned(block, "gx")
    far, near = call(faces_kernel, [(slabs, COUNT + 1) + tile] * 2, [odd, block], scalars=1)
    far = swapped(far, "gy", 1)
    near = swapped(near, "gy", 0)
    nx = layers * slabs
    wide = (2 * ny, nz)
    states, gram = call(
        steps_kernel,
        [(slabs, STEPS, FIELDS, layers) + tile, (share,) + tile],
        [place, odd, drive, moduli, block, far, near],
        [
            (2, FIELDS, nx + 2) + wide, (PAIR, nx) + wide, (2, nx + 2) + wide, (nx,) + wide,
            (2, 6, nx) + wide, (3, nx) + wide, (2, 3) + wide, wide, (2,) + wide, (2, 6) + wide, (3,) + wide,
        ],
        4,
    )
    states = turned(states, "gx")
    count = STEPS * CASES
    width = -(-(count + CASES + 8 * share) // SHARES // 8) * 8
    parts, = call(
        project_kernel, [(rows, width, modes)], [basis, states, gram, local], [(blocks, count * ny, nz)]
    )
    parts, = call(sum_kernel, [(depth, width, modes)], [turned(parts, "gy")])
    parts, = call(sum_kernel, [(SHARES * slabs, width, modes)], [turned(parts, "gz")])
    groups = [
        [(a * rows + 2 * h + core) * depth + z for a in range(slabs) for h in range(rows // 2)]
        for core in range(2)
        for z in range(depth)
    ]
    parts = lax.all_to_all(parts, ("gx", "gy", "gz"), 0, 0, tiled=True, axis_index_groups=groups)
    held = (comps, CASES, layers) + tile
    displacement, modes_out, coefficients, factors = call(
        lambda *refs: finish_kernel(dof_weight, *refs),
        [held, held, (STEPS, 2, CASES, modes), (STEPS, CASES, CASES)],
        [parts, basis, states],
        [(2, blocks, CASES * ny, nz), held],
        copies=comps * CASES + comps,
        outs_away=2,
    )
    return displacement, modes_out, coefficients.transpose(0, 1, 3, 2), factors


def solution(mesh):
    in_specs = (
        P("gx", None, "gy", "gz", None),
        P(),
        P(),
        P("gx", "gy", "gz"),
        P(),
        P(None, "gx", "gy", "gz"),
        P(),
    )
    out_specs = (P(None, None, "gx", "gy", "gz"), P(None, None, "gx", "gy", "gz"), P(), P())
    return jax.shard_map(
        shards, mesh=mesh, in_specs=in_specs, out_specs=out_specs, check_vma=False
    )
```
